32 devices in a mesh: dp: 2 (over x), expert: 16 (over z, y, core).
Axes of the slice: x: 2, y: 2, z: 4, core: 2. Of those that a mesh axis runs over, the one named last changes fastest.
Arguments:
- tokens: bfloat16 [512, 2048], P('expert', 'dp'), may hold values from -6 to 6
- cotangent: bfloat16 [512, 2048], P('expert', 'dp'), may hold values from -6 to 6
- routes: int32 [512, 8], P('expert'), may hold values from 0 to 15, all different within a row; in each aligned block of 32 rows (0 to 31, 32 to 63, ...) at most 20 rows name the same one
- probs: float32 [512, 8], P('expert'), may hold values from 0.03 to 0.6
- matching: int32 [16], replicated, may hold values from 0 to 15, as said below
- gate_weight: bfloat16 [16, 2048, 1024], P('expert', None, 'dp'), may hold values from -0.125 to 0.125
- up_weight: bfloat16 [16, 2048, 1024], P('expert', None, 'dp'), may hold values from -0.125 to 0.125
- down_weight: bfloat16 [16, 2048, 1024], P('expert', None, 'dp'), may hold values from -0.1875 to 0.1875
Outputs:
- input_grad: bfloat16 [512, 2048], P('expert', 'dp')
- gate_weight_grad: float32 [16, 2048, 1024], P('expert', None, 'dp')
- up_weight_grad: float32 [16, 2048, 1024], P('expert', None, 'dp')
- down_weight_grad: float32 [16, 2048, 1024], P('expert', None, 'dp')
The draws below stay inside these ranges and needn't reach their ends.
Inputs may be any that keep to these rules, and one draw needn't show every extreme that they name: matching pairs the experts: matching[matching[i]] == i and matching[i] != i. `routes`: each token names 8 different experts; within each aligned block of 32 tokens no expert is named by more than 20 tokens.
All inputs are finite; a program needn't handle non-finite values.
Results may differ from the reference program's by a relative error of at most 0.015.
Values may be sent and summed in bfloat16 or wider, within the bound.
A program may use at most 64 MiB of HBM per device.

```python
import math
import jax
import jax.numpy as jnp
import numpy as np
from jax import lax

D = 2048
HID = 1024
TOPK = 8
TOK_DEV = 32
EXPERTS = 16
CAP = 20
TOKENS = 512
N_DP = 2
N_EXPERT = 16


def draw_matching(key, part):
    order = jax.random.permutation(key, EXPERTS).astype(jnp.int32)
    first = order[0::2]
    second = order[1::2]
    paired = jnp.zeros((EXPERTS,), jnp.int32).at[first].set(second).at[second].set(first)
    return paired.astype(jnp.int32)


def block_scale(stream_key, dims, cuts, low, top_value):
    gain, own = 1.0, jax.random.fold_in(stream_key, 6)
    for position, shards_of in cuts:
        draws = jnp.exp(jax.random.uniform(jax.random.fold_in(own, position), (shards_of,), jnp.float32, low / len(cuts), top_value / len(cuts)))
        gain = gain * jnp.repeat(draws, dims[position] // shards_of).reshape([-1 if axis == position else 1 for axis in range(len(dims))])
    return gain


def assign_block(own_key, own, number, rows, amount, top, most, slope):
    ranking = jax.random.permutation(own_key, amount)
    heavy_load, common = load_shares(amount, rows * top, most, slope, True), load_shares(amount, rows * top, most, slope, False)
    places = jnp.arange(amount)

    def named(sizes, turn):
        used = int((sizes > 0).sum())
        fixed = max(1, used // 4)
        passed = fixed + (places - fixed + turn * (used - fixed)) % max(1, amount - fixed)
        return jnp.zeros((amount,), jnp.int32).at[ranking[jnp.where(places < fixed, places, passed)]].set(jnp.asarray(sizes, jnp.int32))

    sizes = jnp.where(number % 4 == 0, named(heavy_load, number // 4), named(common, number - number // 4 - 1))
    mixed = jax.random.permutation(jax.random.fold_in(own, 3), amount)
    source_of, taker = mixed[0:amount // 2 * 2:2], mixed[1:amount // 2 * 2:2]
    margin = jnp.minimum(sizes[source_of] - 1, most - sizes[taker]) // 2
    margin = jnp.where((source_of == ranking[0]) | (taker == ranking[0]) | (sizes[taker] == 0), 0, jnp.maximum(margin, 0))
    passed = jax.random.randint(jax.random.fold_in(own, 4), (amount // 2,), 0, 1 << 20) % (margin + 1)
    sizes = sizes.at[source_of].add(-passed).at[taker].add(passed)
    labels = jnp.searchsorted(jnp.cumsum(sizes), jnp.arange(rows * top), side="right").astype(jnp.int32)
    grid = labels.reshape(top, rows).T
    grid = grid[jax.random.permutation(jax.random.fold_in(own, 1), rows)]
    turn = jax.random.randint(jax.random.fold_in(own, 2), (rows, 1), 0, top)
    return jnp.take_along_axis(grid, (jnp.arange(top)[None, :] + turn) % top, axis=1)


def load_shares(count, total, most, skew, full):
    portions = [(1 << 20) // math.isqrt(grade ** skew) + 1 for grade in range(1, count + 1)]
    largest = most if full else min(most, max(-(-total // count), total * portions[0] // sum(portions)))
    least = 1 if total - largest >= count - 1 else 0
    holding, spare = [largest] + [least] * (count - 1), total - largest - least * (count - 1)
    while spare > 0:
        free = [i for i in range(1, count) if holding[i] < largest] or [i for i in range(1, count) if holding[i] < most]
        pool, left = sum([portions[i] for i in free]), spare
        for i in free:
            addition = min(most - holding[i], max(1, left * portions[i] // pool), spare)
            holding[i] = holding[i] + addition
            spare = spare - addition
    return np.array(holding)


def normal_values(key, extent, deviation, bound, split=(), kind=jnp.bfloat16):
    drawn = deviation * jax.random.normal(key, extent, jnp.float32)
    if split:
        drawn = drawn * block_scale(key, extent, split, -0.22, 0.18)
    return jnp.clip(drawn, -bound, bound).astype(kind)


def setup_inputs(seed: int = 0) -> dict:
    arg_keys = jax.random.split(jax.random.key(seed), 9)
    tokens = normal_values(arg_keys[0], (TOKENS, D), 1.0, 6.0, ((0, 16), (1, 2)))
    cotangent = normal_values(arg_keys[1], (TOKENS, D), 1.0, 6.0, ((0, 16), (1, 2)))
    routes_keys = jax.random.split(jax.random.fold_in(arg_keys[2], 1), TOKENS // TOK_DEV)
    routes_turns = jax.random.permutation(jax.random.fold_in(arg_keys[2], 3), TOKENS // TOK_DEV)
    routes = jax.vmap(lambda own, number: assign_block(jax.random.fold_in(arg_keys[2], 2), own, number, TOK_DEV, EXPERTS, TOPK, CAP, 2))(routes_keys, routes_turns).reshape((TOKENS, TOPK))
    probs = jnp.clip(jnp.exp(math.log(0.6) - 2.9957323 * jax.random.uniform(arg_keys[3], (TOKENS, TOPK), jnp.float32) ** block_scale(arg_keys[3], (TOKENS, TOPK), ((0, 16),), -0.2, 0.2)), 0.03, 0.6)
    matching = draw_matching(jax.random.fold_in(arg_keys[8], 71), 0)
    gate_weight = normal_values(arg_keys[5], (EXPERTS, D, HID), D ** -0.5, 0.125, ((0, 16), (2, 2)))
    up_weight = normal_values(arg_keys[6], (EXPERTS, D, HID), D ** -0.5, 0.125, ((0, 16), (2, 2)))
    down_weight = normal_values(arg_keys[7], (EXPERTS, D, HID), HID ** -0.5, 0.1875, ((0, 16), (2, 2)))
    return dict(tokens=tokens, cotangent=cotangent, routes=routes, probs=probs, matching=matching, gate_weight=gate_weight, up_weight=up_weight, down_weight=down_weight)


def reference(tokens, cotangent, routes, probs, matching, gate_weight, up_weight, down_weight):
    pair_total = TOKENS * TOPK
    width = N_EXPERT * CAP
    pair_expert = routes.reshape(pair_total).astype(jnp.int32)
    onehot = (pair_expert[:, None] == jnp.arange(EXPERTS, dtype=jnp.int32)[None, :]).astype(jnp.int32)
    running = jnp.cumsum(onehot.reshape(N_EXPERT, TOK_DEV * TOPK, EXPERTS), axis=1).reshape(pair_total, EXPERTS)
    rank = jnp.sum(onehot * running, axis=1) - 1
    source = jnp.arange(pair_total, dtype=jnp.int32) // (TOK_DEV * TOPK)
    slot = (pair_expert * width + source * CAP + rank).astype(jnp.int32)
    index = jnp.full((EXPERTS * width,), pair_total, jnp.int32).at[slot].set(jnp.arange(pair_total, dtype=jnp.int32))
    index = index.reshape(EXPERTS, width)
    pair_in = jnp.concatenate([jnp.repeat(tokens, TOPK, axis=0), jnp.zeros((1, D), jnp.bfloat16)], axis=0)
    scaled = jnp.repeat(cotangent.astype(jnp.float32), TOPK, axis=0) * probs.reshape(pair_total, 1)
    pair_out = jnp.concatenate([scaled.astype(jnp.bfloat16), jnp.zeros((1, D), jnp.bfloat16)], axis=0)
    slice_width = HID // N_DP
    contract_rows = (((0,), (0,)), ((), ()))

    def one_expert(carry, stuff):
        rows, w_gate, w_up, w_down = stuff
        inputs = pair_in[rows]
        grads = pair_out[rows]
        gate = jnp.dot(inputs, w_gate, preferred_element_type=jnp.float32)
        upper = jnp.dot(inputs, w_up, preferred_element_type=jnp.float32)
        sig = jax.nn.sigmoid(gate)
        hidden = (gate * sig * upper).astype(jnp.bfloat16)
        hidden_back = jnp.dot(grads, w_down, preferred_element_type=jnp.float32)
        up_back = (hidden_back * gate * sig).astype(jnp.bfloat16)
        gate_back = (hidden_back * upper * sig * (1.0 + gate * (1.0 - sig))).astype(jnp.bfloat16)
        gate_sum = lax.dot_general(inputs, gate_back, contract_rows, preferred_element_type=jnp.float32)
        up_sum = lax.dot_general(inputs, up_back, contract_rows, preferred_element_type=jnp.float32)
        down_sum = lax.dot_general(grads, hidden, contract_rows, preferred_element_type=jnp.float32)
        gate_slices = gate_back.astype(jnp.float32).reshape(width, N_DP, slice_width)
        up_slices = up_back.astype(jnp.float32).reshape(width, N_DP, slice_width)
        wg_slices = w_gate.astype(jnp.float32).reshape(D, N_DP, slice_width)
        wu_slices = w_up.astype(jnp.float32).reshape(D, N_DP, slice_width)
        slice_part = jnp.einsum("rsh,dsh->rsd", gate_slices, wg_slices) + jnp.einsum("rsh,dsh->rsd", up_slices, wu_slices)
        pair_back = jnp.sum(slice_part.astype(jnp.bfloat16).astype(jnp.float32), axis=1)
        carry = carry.at[rows].add(pair_back)
        return carry, (gate_sum, up_sum, down_sum)

    start = jnp.zeros((pair_total + 1, D), jnp.float32)
    carry, sums = lax.scan(one_expert, start, (index, gate_weight, up_weight, down_weight))
    input_grad = jnp.sum(carry[:pair_total].reshape(TOKENS, TOPK, D), axis=1).astype(jnp.bfloat16)
    gate_sums, up_sums, down_sums = sums
    return (input_grad, jnp.take(gate_sums, matching, axis=0), jnp.take(up_sums, matching, axis=0), jnp.take(down_sums, matching, axis=0))
```

```python
import functools
import math

import jax
import jax.numpy as jnp
from jax import lax
from jax.experimental import pallas as pl
from jax.experimental.pallas import tpu as pltpu
from jax.sharding import PartitionSpec as P

contract_rows = (((0,), (0,)), ((), ()))
contract_cols = (((1,), (1,)), ((), ()))
MESH = pl.DeviceIdType.MESH
KINDS = 3
LANES = 128
CHUNKS = 2


def bit_count(size):
    return size.bit_length() - 1


def flipped(index, bit):
    step = 2**bit
    return index + step * (1 - 2 * ((index // step) % 2))


def gather_orders(expert_bits, dp_bits):
    far = [("expert", b) for b in range(expert_bits - 1, 1, -1)]
    mid = [("expert", 1)]
    last = [("expert", 0)]
    across = [("dp", b) for b in range(dp_bits)]
    return (
        far + across + mid + last,
        across + far + mid + last,
        far + mid + across + last,
        mid + far + across + last,
        far + mid + last,
    )


def reduce_orders(expert_bits, dp_bits):
    far = [("expert", b) for b in range(2, expert_bits)]
    mid = [("expert", 1)]
    near = [("expert", 0)]
    across = [("dp", b) for b in range(dp_bits - 1, -1, -1)]
    return (near + across + mid + far, near + mid + across + far)


def reduce_shapes(order, expert_bits, dp_bits, rows, width):
    left_e, left_d = expert_bits, dp_bits
    shapes = []
    for axis, _ in order:
        if axis == "expert":
            left_e -= 1
        else:
            left_d -= 1
        shapes.append((2,) * left_e + (rows, width * 2**left_d))
    return shapes


class Plan:
    def __init__(self, n_expert, n_dp, tok_rows, width, top_count, hidden):
        self.n_expert, self.n_dp = n_expert, n_dp
        self.expert_bits, self.dp_bits = bit_count(n_expert), bit_count(n_dp)
        self.tok_rows, self.width, self.hidden = tok_rows, width, hidden
        self.top_count = top_count
        self.model = width * n_dp
        self.total = n_expert * tok_rows
        self.capacity = max(2, 5 * tok_rows * top_count // (4 * n_expert))
        self.blocks = 16 // math.gcd(16, self.capacity)
        self.groups = n_expert // self.blocks
        self.group_slots = self.blocks * self.capacity
        self.group_toks = self.blocks * tok_rows
        self.slots = self.groups * self.group_slots
        self.half = n_expert // 2
        self.chunks = CHUNKS
        self.chunk_groups = self.groups // self.chunks
        self.col_tiles = hidden // LANES
        self.row_split = max(1, self.half // (self.chunk_groups * self.col_tiles))
        unit = 16 * self.row_split
        self.group_rows = -(-KINDS * self.group_slots // unit) * unit
        self.piece_rows = self.group_rows // self.row_split
        self.chunk_toks = self.total // self.chunks
        self.steps = self.expert_bits + self.dp_bits
        self.row_parts = 2 if 2**self.steps <= 128 else 1


def comm_kernel(
    p,
    crossing,
    match,
    tokens,
    cotangent,
    routes,
    probs,
    h_gate,
    h_up,
    h_down,
    landed,
    out_rows,
    out_grads,
    result,
    *scratch,
):
    n, half = p.n_expert, p.half
    steps, chunks = p.steps, p.chunks
    halves = 2
    sums = [scratch[i * steps : (i + 1) * steps] for i in range(halves)]
    came = [scratch[(halves + i) * steps : (halves + i + 1) * steps] for i in range(halves)]
    rest = scratch[2 * halves * steps :]
    arrived = rest[:chunks]
    swapped = rest[chunks : 2 * chunks]
    staged = rest[2 * chunks : 3 * chunks]
    ordered = rest[3 * chunks : 4 * chunks]
    (
        all_tok,
        all_cot,
        all_routes,
        all_probs,
        w_gate,
        w_up,
        w_down,
        weights,
        places,
        p_weights,
        p_places,
        scaled,
        backs,
        packed,
        part,
        x_rows,
        x_grads,
        summed,
        gsend,
        grecv,
        msend,
        mrecv,
        own,
        wsem,
        send1,
        recv1,
        send2,
        recv2,
        send3,
        recv3,
        stay1,
        stay3,
        rsend,
        rrecv,
        osem,
    ) = rest[4 * chunks :]
    e = lax.axis_index("expert")
    d = lax.axis_index("dp")
    h = e % half
    base = e - h
    rows_half = p.tok_rows // 2
    part_rows = p.tok_rows // p.row_parts
    width = p.width

    def peer(axis, bit):
        if axis == "expert":
            return (d, flipped(e, bit))
        return (flipped(d, bit), e)

    def origin(order, mask):
        at_e, at_d = e, d
        for k, (axis, bit) in enumerate(order):
            if mask >> k & 1:
                if axis == "expert":
                    at_e = flipped(at_e, bit)
                else:
                    at_d = flipped(at_d, bit)
        return at_e, at_d

    orders = gather_orders(p.expert_bits, p.dp_bits)
    sources = (
        (tokens, all_tok, 0, orders[0]),
        (cotangent, all_cot, 0, orders[1]),
        (tokens, all_tok, 1, orders[2]),
        (cotangent, all_cot, 1, orders[3]),
    )[: 2 * p.row_parts]

    def block(dst, index, at_e, at_d):
        row = pl.multiple_of(at_e * p.tok_rows + index * part_rows, part_rows)
        col = pl.multiple_of(at_d * width, width)
        return dst.at[pl.ds(row, part_rows), pl.ds(col, width)]

    metas = ((routes, all_routes), (probs, all_probs))
    locals_ = []
    for i, (src, dst) in enumerate(((tokens, all_tok), (cotangent, all_cot))):
        row = pl.multiple_of(e * p.tok_rows, p.tok_rows)
        col = pl.multiple_of(d * width, width)
        c = pltpu.make_async_copy(
            src, dst.at[pl.ds(row, p.tok_rows), pl.ds(col, width)], own.at[i]
        )
        c.start()
        locals_.append(c)
    for i, (src, dst) in enumerate(metas):
        c = pltpu.make_async_copy(src, dst.at[e], own.at[2 + i])
        c.start()
        locals_.append(c)

    barrier = pltpu.get_barrier_semaphore()

    @pl.loop(1, half)
    def _(o):
        pl.semaphore_signal(
            barrier, inc=1, device_id=(d, base + (h + o) % half), device_id_type=MESH
        )

    mirror = (d, (e + half) % n)
    pl.semaphore_signal(barrier, inc=1, device_id=mirror, device_id_type=MESH)
    for b in range(p.dp_bits):
        pl.semaphore_signal(barrier, inc=1, device_id=(flipped(d, b), e), device_id_type=MESH)
    pl.semaphore_wait(barrier, half + p.dp_bits)

    def flight(i, mask, k):
        src, dst, index, order = sources[i]
        at = block(dst, index, *origin(order, mask))
        if mask == 0:
            src = src.at[pl.ds(index * part_rows, part_rows)]
        else:
            src = at
        got = mask + 2**k
        return pltpu.make_async_remote_copy(
            src_ref=src,
            dst_ref=at,
            send_sem=gsend.at[i, got],
            recv_sem=grecv.at[i, got],
            device_id=peer(*order[k]),
            device_id_type=MESH,
        )

    def meta_flight(i, mask, k):
        src, dst = metas[i]
        at = dst.at[origin(orders[4], mask)[0]]
        got = mask + 2**k
        return pltpu.make_async_remote_copy(
            src_ref=src if mask == 0 else at,
            dst_ref=at,
            send_sem=msend.at[i, got],
            recv_sem=mrecv.at[i, got],
            device_id=peer(*orders[4][k]),
            device_id_type=MESH,
        )

    flights, meta_flights = {}, {}

    def send_on(i, mask):
        top = mask.bit_length()
        for k in range(top, steps):
            c = flight(i, mask, k)
            c.start()
            flights[i, mask + 2**k] = c

    def meta_on(i, mask):
        for k in range(mask.bit_length(), p.expert_bits):
            c = meta_flight(i, mask, k)
            c.start()
            meta_flights[i, mask + 2**k] = c

    for i in range(len(sources)):
        send_on(i, 0)
    for i in range(len(metas)):
        meta_on(i, 0)
    loads = []
    for i, (src, dst) in enumerate(((h_gate, w_gate), (h_up, w_up), (h_down, w_down))):
        c = pltpu.make_async_copy(src, dst, wsem.at[i])
        c.start()
        loads.append(c)

    def turn(mask):
        top = 2 ** (mask.bit_length() - 1)
        return (mask - top, top)

    inner = sorted(range(1, 2 ** (steps - 1)), key=turn)
    meta_masks = sorted(range(1, 2**p.expert_bits), key=turn)
    for count, mask in enumerate(inner):
        for i in range(len(sources)):
            flights[i, mask].wait_recv()
            send_on(i, mask)
        if count < len(meta_masks):
            for i in range(len(metas)):
                meta_flights[i, meta_masks[count]].wait_recv()
                meta_on(i, meta_masks[count])
    for mask in meta_masks[len(inner) :]:
        for i in range(len(metas)):
            meta_flights[i, mask].wait_recv()
            meta_on(i, mask)
    for c in locals_:
        c.wait()

    partner = match[e]
    tok = p.tok_rows
    at = lax.broadcasted_iota(jnp.int32, (tok, tok), 0)
    to = lax.broadcasted_iota(jnp.int32, (tok, tok), 1)

    @pl.loop(0, n)
    def _(b):
        r = all_routes[b]
        q = all_probs[b]
        rows = pl.ds(pl.multiple_of(b * tok, tok), tok)
        start = ((b % p.blocks) * p.capacity).astype(jnp.float32)
        for who, w_ref, s_ref in ((e, weights, places), (partner, p_weights, p_places)):
            hit = r == who
            w = jnp.sum(jnp.where(hit, q, 0.0), axis=0, keepdims=True)
            f = jnp.sum(jnp.where(hit, 1.0, 0.0), axis=0, keepdims=True)
            w = jnp.broadcast_to(w, (tok, tok))
            f = jnp.broadcast_to(f, (tok, tok))
            w_col = jnp.sum(jnp.where(at == to, w, 0.0), axis=1, keepdims=True)
            f_col = jnp.sum(jnp.where(at == to, f, 0.0), axis=1, keepdims=True)
            rank = jnp.sum(jnp.where(to < at, f, 0.0), axis=1, keepdims=True)
            s_col = jnp.where(f_col > 0.5, rank + start, -1.0)
            w_ref[rows, :] = jnp.broadcast_to(w_col, (tok, LANES))
            s_ref[rows, :] = jnp.broadcast_to(s_col, (tok, LANES))

    def picker(s_ref, g):
        place = s_ref[g * p.group_toks : (g + 1) * p.group_toks, :]
        lane = lax.broadcasted_iota(jnp.int32, place.shape, 1).astype(jnp.float32)
        hot = jnp.where(place == lane, 1.0, 0.0)
        return jnp.transpose(hot)[: p.group_slots].astype(jnp.bfloat16)

    for mask in range(2 ** (steps - 1), 2**steps):
        for i in range(len(sources)):
            flights[i, mask].wait_recv()
    for c in loads:
        c.wait()

    tile_rows = min(256, p.chunk_toks)
    tile_cols = min(256, p.hidden)

    def forward(c):
        @pl.loop(0, p.chunk_toks // tile_rows)
        def _(t):
            first_row = pl.multiple_of(c * p.chunk_toks + t * tile_rows, tile_rows)
            rows = pl.ds(first_row, tile_rows)
            w = weights[rows, :][:, :1]
            scaled[...] = (all_cot[rows, :].astype(jnp.float32) * w).astype(jnp.bfloat16)

            @pl.loop(0, p.hidden // tile_cols)
            def _(u):
                cols = pl.ds(pl.multiple_of(u * tile_cols, tile_cols), tile_cols)
                x = all_tok[rows, :]
                gate = jnp.dot(x, w_gate[0, :, cols], preferred_element_type=jnp.float32)
                upper = jnp.dot(x, w_up[0, :, cols], preferred_element_type=jnp.float32)
                back = jnp.dot(
                    scaled[...], w_down[0, :, cols], preferred_element_type=jnp.float32
                )
                sig = jax.nn.sigmoid(gate)
                backs[0, rows, cols] = (
                    back * upper * sig * (1.0 + gate * (1.0 - sig))
                ).astype(jnp.bfloat16)
                backs[1, rows, cols] = (back * gate * sig).astype(jnp.bfloat16)
                backs[2, rows, cols] = (gate * sig * upper).astype(jnp.bfloat16)

    def pack(c):
        for gl in range(p.chunk_groups):
            g = c * p.chunk_groups + gl
            pick = picker(places, g)
            rows = slice(g * p.group_toks, (g + 1) * p.group_toks)
            kinds = [
                jnp.dot(pick, backs[k, rows, :], preferred_element_type=jnp.float32).astype(
                    jnp.bfloat16
                )
                for k in range(KINDS)
            ]
            spare = p.group_rows - KINDS * p.group_slots
            if spare:
                kinds.append(jnp.zeros((spare, p.hidden), jnp.bfloat16))
            whole = jnp.concatenate(kinds, axis=0)
            for t in range(p.col_tiles):
                j = (gl * p.col_tiles + t) * p.row_split
                piece = whole[:, t * LANES : (t + 1) * LANES]
                packed[c, j : j + p.row_split] = piece.reshape(
                    p.row_split, p.piece_rows, LANES
                )

    def spread(c, o):
        to_h = (h + o) % half
        return pltpu.make_async_remote_copy(
            src_ref=packed.at[c, to_h],
            dst_ref=arrived[c].at[h],
            send_sem=send1.at[c, o],
            recv_sem=recv1.at[c, o],
            device_id=(d, base + to_h),
            device_id_type=MESH,
        )

    def swap(c):
        return pltpu.make_async_remote_copy(
            src_ref=staged[c],
            dst_ref=swapped[c],
            send_sem=send2.at[c],
            recv_sem=recv2.at[c],
            device_id=mirror,
            device_id_type=MESH,
        )

    def collect(c, o):
        to_h = (h + o) % half
        return pltpu.make_async_remote_copy(
            src_ref=ordered[c].at[to_h],
            dst_ref=landed.at[c, h],
            send_sem=send3.at[c, o],
            recv_sem=recv3.at[c, o],
            device_id=(d, base + to_h),
            device_id_type=MESH,
        )

    def stay_first(c):
        return pltpu.make_async_copy(packed.at[c, h], arrived[c].at[h], stay1.at[c])

    def stay_last(c):
        return pltpu.make_async_copy(ordered[c].at[h], landed.at[c, h], stay3.at[c])

    def begin(c):
        forward(c)
        pack(c)
        stay_first(c).start()

        @pl.loop(1, half)
        def _(o):
            spread(c, o).start()

    def cross_list(start):
        flags, before, count = [], [], 0
        for i in range(half):
            m = match[start + i]
            inside = (m >= start) & (m < start + half)
            flag = jnp.where(inside, 0, 1)
            flags.append(flag)
            before.append(count)
            count = count + flag
        return flags, before

    def cross_at(listed, k):
        flags, before = listed
        found = 0
        for i in range(half):
            found = found + jnp.where((flags[i] == 1) & (before[i] == k), i, 0)
        return found

    other = (base + half) % n
    full = crossing == half

    def swap_on(c):
        stay_first(c).wait()

        @pl.loop(1, half)
        def _(o):
            spread(c, o).wait_recv()

        if full:
            staged[c][...] = arrived[c][...]
        else:
            mine = cross_list(base)
            for k in range(crossing):
                staged[c][k] = arrived[c][cross_at(mine, k)]
        swap(c).start()

    def collect_on(c):
        swap(c).wait_recv()
        theirs = None if full else cross_list(other)
        for i in range(half):
            m = match[base + i]
            inside = (m >= base) & (m < base + half)
            near = arrived[c][jnp.where(inside, m - base, 0)]
            if full:
                far_at = jnp.where(inside, 0, m - other)
            else:
                far_at = 0
                for k in range(half):
                    far_at = far_at + jnp.where(m - other == k, theirs[1][k], 0)
                far_at = jnp.where(inside, 0, far_at)
            far = swapped[c][far_at]
            ordered[c][i] = jnp.where(inside, near, far)
        stay_last(c).start()

        @pl.loop(1, half)
        def _(o):
            collect(c, o).start()

    r_orders = reduce_orders(p.expert_bits, p.dp_bits)
    r_flights = [[], []]

    def split(i, s):
        axis, bit = r_orders[i][s]
        if s == 0:
            ref, rows = part, pl.ds(i * rows_half, rows_half)
        else:
            ref, rows = sums[i][s - 1], slice(None)
        left = [b for a, b in r_orders[i][s:] if a == "expert"]
        left = sorted(left, reverse=True)
        if axis == "expert":
            mine = (e // 2**bit) % 2
            spot = left.index(bit)

            def where(v):
                return tuple(
                    [slice(None)] * spot + [v] + [slice(None)] * (len(left) - spot - 1)
                ) + (rows, slice(None))

            return ref, where(mine), where(1 - mine)
        mine = (d // 2**bit) % 2
        span = 2**bit * width
        head = (slice(None),) * len(left) + (rows,)
        keep = head + (pl.ds(pl.multiple_of(mine * span, LANES), span),)
        give = head + (pl.ds(pl.multiple_of((1 - mine) * span, LANES), span),)
        return ref, keep, give

    def start_step(i, s):
        ref, _, give = split(i, s)
        c = pltpu.make_async_remote_copy(
            src_ref=ref.at[give],
            dst_ref=came[i][s],
            send_sem=rsend.at[i, s],
            recv_sem=rrecv.at[i, s],
            device_id=peer(*r_orders[i][s]),
            device_id_type=MESH,
        )
        c.start()
        r_flights[i].append(c)

    def end_step(i, s):
        ref, keep, _ = split(i, s)
        r_flights[i][s].wait_recv()
        total = ref[keep].astype(jnp.float32) + came[i][s][...].astype(jnp.float32)
        sums[i][s][...] = total.astype(sums[i][s].dtype)

    def next_step(s):
        for i in range(halves):
            end_step(i, s)
            if s + 1 < steps:
                start_step(i, s + 1)

    def pack_rows(src, dst, w_ref):
        for g in range(p.groups):
            pick = picker(p_places, g)
            rows = slice(g * p.group_toks, (g + 1) * p.group_toks)
            at_rows = slice(g * p.group_slots, (g + 1) * p.group_slots)
            span = min(512, p.model)
            for t in range(0, p.model, span):
                x = src[rows, t : t + span]
                if w_ref is not None:
                    x = (x.astype(jnp.float32) * w_ref[rows, :][:, :1]).astype(jnp.bfloat16)
                dst[at_rows, t : t + span] = jnp.dot(
                    pick, x, preferred_element_type=jnp.float32
                ).astype(jnp.bfloat16)

    for c in range(chunks):
        begin(c)
    swap_on(0)
    tile = min(512, p.model)
    for t in range(0, p.model, tile):
        piece = lax.dot_general(
            backs[0], w_gate[0, t : t + tile], contract_cols, preferred_element_type=jnp.float32
        )
        piece += lax.dot_general(
            backs[1], w_up[0, t : t + tile], contract_cols, preferred_element_type=jnp.float32
        )
        shape = part.shape[:-1] + (tile,)
        part[..., t : t + tile] = piece.astype(part.dtype).reshape(shape)
    for i in range(halves):
        start_step(i, 0)
    for c in range(1, chunks):
        swap_on(c)
    pack_rows(all_tok, x_rows, None)
    row_out = pltpu.make_async_copy(x_rows, out_rows, osem.at[0])
    row_out.start()
    next_step(0)
    pack_rows(all_cot, x_grads, p_weights)
    grad_out = pltpu.make_async_copy(x_grads, out_grads, osem.at[1])
    grad_out.start()
    next_step(1)
    collect_on(0)
    for s in range(2, steps - 1):
        next_step(s)
    for c in range(1, chunks):
        collect_on(c)
    next_step(steps - 1)
    for i in range(halves):
        summed[pl.ds(i * rows_half, rows_half), :] = sums[i][steps - 1][...]
    result_out = pltpu.make_async_copy(summed, result, osem.at[2])
    result_out.start()

    for c in flights.values():
        c.wait_send()
    for c in meta_flights.values():
        c.wait_send()
    for f in r_flights:
        for c in f:
            c.wait_send()
    row_out.wait()
    grad_out.wait()
    result_out.wait()
    for c in range(chunks):
        stay_last(c).wait()
        swap(c).wait_send()

        @pl.loop(1, half)
        def _(o):
            spread(c, o).wait_send()
            collect(c, o).wait_send()
            collect(c, o).wait_recv()


def communicate(p, crossing, call_id, operands):
    dtype = operands[1].dtype
    reduce_buffers = []
    for order in reduce_orders(p.expert_bits, p.dp_bits):
        for shape in reduce_shapes(order, p.expert_bits, p.dp_bits, p.tok_rows // 2, p.width):
            reduce_buffers.append(pltpu.VMEM(shape, dtype))
    piece = (p.piece_rows, LANES)
    weight = operands[-1].shape
    dma = pltpu.SemaphoreType.DMA
    steps, chunks, half = p.steps, p.chunks, p.half
    scratch = (
        reduce_buffers
        + reduce_buffers
        + [pltpu.VMEM((half,) + piece, dtype)] * chunks
        + [pltpu.VMEM((crossing,) + piece, dtype)] * (2 * chunks)
        + [pltpu.VMEM((half,) + piece, dtype)] * chunks
        + [
            pltpu.VMEM((p.total, p.model), dtype),
            pltpu.VMEM((p.total, p.model), dtype),
            pltpu.VMEM((p.n_expert, p.top_count, p.tok_rows), jnp.int32),
            pltpu.VMEM((p.n_expert, p.top_count, p.tok_rows), jnp.float32),
            pltpu.VMEM(weight, dtype),
            pltpu.VMEM(weight, dtype),
            pltpu.VMEM(weight, dtype),
            pltpu.VMEM((p.total, LANES), jnp.float32),
            pltpu.VMEM((p.total, LANES), jnp.float32),
            pltpu.VMEM((p.total, LANES), jnp.float32),
            pltpu.VMEM((p.total, LANES), jnp.float32),
            pltpu.VMEM((min(256, p.chunk_toks), p.model), dtype),
            pltpu.VMEM((KINDS, p.total, p.hidden), dtype),
            pltpu.VMEM((chunks, half) + piece, dtype),
            pltpu.VMEM((2,) * p.expert_bits + (p.tok_rows, p.model), dtype),
            pltpu.VMEM((p.slots, p.model), dtype),
            pltpu.VMEM((p.slots, p.model), dtype),
            pltpu.VMEM((p.tok_rows, p.width), dtype),
            dma((2 * p.row_parts, 2**steps)),
            dma((2 * p.row_parts, 2**steps)),
            dma((2, p.n_expert)),
            dma((2, p.n_expert)),
            dma((4,)),
            dma((3,)),
            dma((chunks, half)),
            dma((chunks, half)),
            dma((chunks,)),
            dma((chunks,)),
            dma((chunks, half)),
            dma((chunks, half)),
            dma((chunks,)),
            dma((chunks,)),
            dma((2, steps)),
            dma((2, steps)),
            dma((3,)),
        ]
    )
    anywhere = pl.BlockSpec(memory_space=pl.ANY)
    return pl.pallas_call(
        functools.partial(comm_kernel, p, crossing),
        out_shape=(
            jax.ShapeDtypeStruct((chunks, half) + piece, dtype),
            jax.ShapeDtypeStruct((p.slots, p.model), dtype),
            jax.ShapeDtypeStruct((p.slots, p.model), dtype),
            jax.ShapeDtypeStruct((p.tok_rows, p.width), dtype),
        ),
        in_specs=[pl.BlockSpec(memory_space=pltpu.SMEM)] + [anywhere] * 7,
        out_specs=[anywhere] * 4,
        scratch_shapes=scratch,
        compiler_params=pltpu.CompilerParams(
            collective_id=call_id, has_side_effects=True, vmem_limit_bytes=64 * 2**20 - 2**16
        ),
    )(*operands)


def final_kernel(p, landed, rows, grads, summed, g_gate, g_up, g_down, out, acts):
    @pl.when(pl.program_id(0) == 0)
    def _():
        out[...] = summed[...]
        for c in range(p.chunks):
            for gl in range(p.chunk_groups):
                at = (c * p.chunk_groups + gl) * p.group_slots
                for t in range(p.col_tiles):
                    j = (gl * p.col_tiles + t) * p.row_split
                    piece = landed[c, j : j + p.row_split].reshape(p.group_rows, LANES)
                    for k in range(KINDS):
                        acts[k, at : at + p.group_slots, t * LANES : (t + 1) * LANES] = piece[
                            k * p.group_slots : (k + 1) * p.group_slots
                        ]

    x = rows[...]
    g_gate[0] = lax.dot_general(x, acts[0], contract_rows, preferred_element_type=jnp.float32)
    g_up[0] = lax.dot_general(x, acts[1], contract_rows, preferred_element_type=jnp.float32)
    g_down[0] = lax.dot_general(
        grads[...], acts[2], contract_rows, preferred_element_type=jnp.float32
    )


def finish(p, landed, rows, grads, summed):
    tile = min(256, p.model)
    wide = pl.BlockSpec((p.slots, tile), lambda i: (0, i))
    grad = pl.BlockSpec((1, tile, p.hidden), lambda i: (0, i, 0))
    grad_shape = jax.ShapeDtypeStruct((1, p.model, p.hidden), jnp.float32)
    whole = pl.BlockSpec(landed.shape, lambda i: (0, 0, 0, 0))
    small = pl.BlockSpec(summed.shape, lambda i: (0, 0))
    return pl.pallas_call(
        functools.partial(final_kernel, p),
        out_shape=(
            grad_shape,
            grad_shape,
            grad_shape,
            jax.ShapeDtypeStruct(summed.shape, summed.dtype),
        ),
        grid=(p.model // tile,),
        in_specs=[whole, wide, wide, small],
        out_specs=[grad, grad, grad, small],
        scratch_shapes=[pltpu.VMEM((KINDS, p.slots, p.hidden), landed.dtype)],
    )(landed, rows, grads, summed)


def local(n_expert, n_dp, tokens, cotangent, routes, probs, matching, w_gate, w_up, w_down):
    tok_rows, top_count = routes.shape
    p = Plan(n_expert, n_dp, tok_rows, tokens.shape[1], top_count, w_gate.shape[2])
    operands = (matching, tokens, cotangent, routes.T, probs.T, w_gate, w_up, w_down)
    landed, rows, grads, summed = communicate(p, p.half, 0, operands)
    g_gate, g_up, g_down, input_grad = finish(p, landed, rows, grads, summed)
    return input_grad, g_gate, g_up, g_down


def solution(mesh):
    weights = P("expert", None, "dp")
    return jax.shard_map(
        functools.partial(local, mesh.shape["expert"], mesh.shape["dp"]),
        mesh=mesh,
        in_specs=(
            P("expert", "dp"),
            P("expert", "dp"),
            P("expert", None),
            P("expert", None),
            P(),
            weights,
            weights,
            weights,
        ),
        out_specs=(P("expert", "dp"), weights, weights, weights),
        check_vma=False,
    )
```

```python
import functools
import math

import jax
import jax.numpy as jnp
from jax import lax
from jax.experimental import pallas as pl
from jax.experimental.pallas import tpu as pltpu
from jax.sharding import PartitionSpec as P

contract_rows = (((0,), (0,)), ((), ()))
contract_cols = (((1,), (1,)), ((), ()))
MESH = pl.DeviceIdType.MESH
KINDS = 3
LANES = 128
CHUNKS = 2


def bit_count(size):
    return size.bit_length() - 1


def flipped(index, bit):
    step = 2**bit
    return index + step * (1 - 2 * ((index // step) % 2))


def gather_orders(expert_bits, dp_bits):
    far = [("expert", b) for b in range(expert_bits - 1, 1, -1)]
    mid = [("expert", 1)]
    last = [("expert", 0)]
    across = [("dp", b) for b in range(dp_bits)]
    return (
        far + across + mid + last,
        across + far + mid + last,
        far + mid + across + last,
        mid + far + across + last,
        far + mid + last,
    )


def reduce_orders(expert_bits, dp_bits):
    far = [("expert", b) for b in range(2, expert_bits)]
    mid = [("expert", 1)]
    near = [("expert", 0)]
    across = [("dp", b) for b in range(dp_bits - 1, -1, -1)]
    return (near + across + mid + far, near + mid + across + far)


def reduce_shapes(order, expert_bits, dp_bits, rows, width):
    left_e, left_d = expert_bits, dp_bits
    shapes = []
    for axis, _ in order:
        if axis == "expert":
            left_e -= 1
        else:
            left_d -= 1
        shapes.append((2,) * left_e + (rows, width * 2**left_d))
    return shapes


class Plan:
    def __init__(self, n_expert, n_dp, tok_rows, width, top_count, hidden):
        self.n_expert, self.n_dp = n_expert, n_dp
        self.expert_bits, self.dp_bits = bit_count(n_expert), bit_count(n_dp)
        self.tok_rows, self.width, self.hidden = tok_rows, width, hidden
        self.top_count = top_count
        self.model = width * n_dp
        self.total = n_expert * tok_rows
        self.capacity = max(2, 5 * tok_rows * top_count // (4 * n_expert))
        self.blocks = 16 // math.gcd(16, self.capacity)
        self.groups = n_expert // self.blocks
        self.group_slots = self.blocks * self.capacity
        self.group_toks = self.blocks * tok_rows
        self.slots = self.groups * self.group_slots
        self.half = n_expert // 2
        self.chunks = CHUNKS
        self.chunk_groups = self.groups // self.chunks
        self.col_tiles = hidden // LANES
        self.row_split = max(1, self.half // (self.chunk_groups * self.col_tiles))
        unit = 16 * self.row_split
        self.group_rows = -(-KINDS * self.group_slots // unit) * unit
        self.piece_rows = self.group_rows // self.row_split
        self.chunk_toks = self.total // self.chunks
        self.steps = self.expert_bits + self.dp_bits
        self.row_parts = 2 if 2**self.steps <= 128 else 1


def comm_kernel(
    p,
    crossing,
    match,
    tokens,
    cotangent,
    routes,
    probs,
    h_gate,
    h_up,
    h_down,
    landed,
    out_rows,
    out_grads,
    result,
    *scratch,
):
    n, half = p.n_expert, p.half
    steps, chunks = p.steps, p.chunks
    halves = 2
    sums = [scratch[i * steps : (i + 1) * steps] for i in range(halves)]
    came = [scratch[(halves + i) * steps : (halves + i + 1) * steps] for i in range(halves)]
    rest = scratch[2 * halves * steps :]
    arrived = rest[:chunks]
    swapped = rest[chunks : 2 * chunks]
    staged = rest[2 * chunks : 3 * chunks]
    ordered = rest[3 * chunks : 4 * chunks]
    (
        all_tok,
        all_cot,
        all_routes,
        all_probs,
        w_gate,
        w_up,
        w_down,
        weights,
        places,
        p_weights,
        p_places,
        scaled,
        backs,
        packed,
        part,
        x_rows,
        x_grads,
        summed,
        gsend,
        grecv,
        msend,
        mrecv,
        own,
        wsem,
        send1,
        recv1,
        send2,
        recv2,
        send3,
        recv3,
        stay1,
        stay3,
        rsend,
        rrecv,
        osem,
    ) = rest[4 * chunks :]
    e = lax.axis_index("expert")
    d = lax.axis_index("dp")
    h = e % half
    base = e - h
    rows_half = p.tok_rows // 2
    part_rows = p.tok_rows // p.row_parts
    width = p.width

    def peer(axis, bit):
        if axis == "expert":
            return (d, flipped(e, bit))
        return (flipped(d, bit), e)

    def origin(order, mask):
        at_e, at_d = e, d
        for k, (axis, bit) in enumerate(order):
            if mask >> k & 1:
                if axis == "expert":
                    at_e = flipped(at_e, bit)
                else:
                    at_d = flipped(at_d, bit)
        return at_e, at_d

    orders = gather_orders(p.expert_bits, p.dp_bits)
    sources = (
        (tokens, all_tok, 0, orders[0]),
        (cotangent, all_cot, 0, orders[1]),
        (tokens, all_tok, 1, orders[2]),
        (cotangent, all_cot, 1, orders[3]),
    )[: 2 * p.row_parts]

    def block(dst, index, at_e, at_d):
        row = pl.multiple_of(at_e * p.tok_rows + index * part_rows, part_rows)
        col = pl.multiple_of(at_d * width, width)
        return dst.at[pl.ds(row, part_rows), pl.ds(col, width)]

    metas = ((routes, all_routes), (probs, all_probs))
    locals_ = []
    for i, (src, dst) in enumerate(((tokens, all_tok), (cotangent, all_cot))):
        row = pl.multiple_of(e * p.tok_rows, p.tok_rows)
        col = pl.multiple_of(d * width, width)
        c = pltpu.make_async_copy(
            src, dst.at[pl.ds(row, p.tok_rows), pl.ds(col, width)], own.at[i]
        )
        c.start()
        locals_.append(c)
    for i, (src, dst) in enumerate(metas):
        c = pltpu.make_async_copy(src, dst.at[e], own.at[2 + i])
        c.start()
        locals_.append(c)

    barrier = pltpu.get_barrier_semaphore()

    @pl.loop(1, half)
    def _(o):
        pl.semaphore_signal(
            barrier, inc=1, device_id=(d, base + (h + o) % half), device_id_type=MESH
        )

    mirror = (d, (e + half) % n)
    pl.semaphore_signal(barrier, inc=1, device_id=mirror, device_id_type=MESH)
    for b in range(p.dp_bits):
        pl.semaphore_signal(barrier, inc=1, device_id=(flipped(d, b), e), device_id_type=MESH)
    pl.semaphore_wait(barrier, half + p.dp_bits)

    def flight(i, mask, k):
        src, dst, index, order = sources[i]
        at = block(dst, index, *origin(order, mask))
        if mask == 0:
            src = src.at[pl.ds(index * part_rows, part_rows)]
        else:
            src = at
        got = mask + 2**k
        return pltpu.make_async_remote_copy(
            src_ref=src,
            dst_ref=at,
            send_sem=gsend.at[i, got],
            recv_sem=grecv.at[i, got],
            device_id=peer(*order[k]),
            device_id_type=MESH,
        )

    def meta_flight(i, mask, k):
        src, dst = metas[i]
        at = dst.at[origin(orders[4], mask)[0]]
        got = mask + 2**k
        return pltpu.make_async_remote_copy(
            src_ref=src if mask == 0 else at,
            dst_ref=at,
            send_sem=msend.at[i, got],
            recv_sem=mrecv.at[i, got],
            device_id=peer(*orders[4][k]),
            device_id_type=MESH,
        )

    flights, meta_flights = {}, {}

    def send_on(i, mask):
        top = mask.bit_length()
        for k in range(top, steps):
            c = flight(i, mask, k)
            c.start()
            flights[i, mask + 2**k] = c

    def meta_on(i, mask):
        for k in range(mask.bit_length(), p.expert_bits):
            c = meta_flight(i, mask, k)
            c.start()
            meta_flights[i, mask + 2**k] = c

    for i in range(len(sources)):
        send_on(i, 0)
    for i in range(len(metas)):
        meta_on(i, 0)
    loads = []
    for i, (src, dst) in enumerate(((h_gate, w_gate), (h_up, w_up), (h_down, w_down))):
        c = pltpu.make_async_copy(src, dst, wsem.at[i])
        c.start()
        loads.append(c)

    def turn(mask):
        top = 2 ** (mask.bit_length() - 1)
        return (mask - top, top)

    inner = sorted(range(1, 2 ** (steps - 1)), key=turn)
    meta_masks = sorted(range(1, 2**p.expert_bits), key=turn)
    for count, mask in enumerate(inner):
        for i in range(len(sources)):
            flights[i, mask].wait_recv()
            send_on(i, mask)
        if count < len(meta_masks):
            for i in range(len(metas)):
                meta_flights[i, meta_masks[count]].wait_recv()
                meta_on(i, meta_masks[count])
    for mask in meta_masks[len(inner) :]:
        for i in range(len(metas)):
            meta_flights[i, mask].wait_recv()
            meta_on(i, mask)
    for c in locals_:
        c.wait()

    partner = match[e]
    tok = p.tok_rows
    at = lax.broadcasted_iota(jnp.int32, (tok, tok), 0)
    to = lax.broadcasted_iota(jnp.int32, (tok, tok), 1)

    @pl.loop(0, n)
    def _(b):
        r = all_routes[b]
        q = all_probs[b]
        rows = pl.ds(pl.multiple_of(b * tok, tok), tok)
        start = ((b % p.blocks) * p.capacity).astype(jnp.float32)
        for who, w_ref, s_ref in ((e, weights, places), (partner, p_weights, p_places)):
            hit = r == who
            w = jnp.sum(jnp.where(hit, q, 0.0), axis=0, keepdims=True)
            f = jnp.sum(jnp.where(hit, 1.0, 0.0), axis=0, keepdims=True)
            w = jnp.broadcast_to(w, (tok, tok))
            f = jnp.broadcast_to(f, (tok, tok))
            w_col = jnp.sum(jnp.where(at == to, w, 0.0), axis=1, keepdims=True)
            f_col = jnp.sum(jnp.where(at == to, f, 0.0), axis=1, keepdims=True)
            rank = jnp.sum(jnp.where(to < at, f, 0.0), axis=1, keepdims=True)
            s_col = jnp.where(f_col > 0.5, rank + start, -1.0)
            w_ref[rows, :] = jnp.broadcast_to(w_col, (tok, LANES))
            s_ref[rows, :] = jnp.broadcast_to(s_col, (tok, LANES))

    def picker(s_ref, g):
        place = s_ref[g * p.group_toks : (g + 1) * p.group_toks, :]
        lane = lax.broadcasted_iota(jnp.int32, place.shape, 1).astype(jnp.float32)
        hot = jnp.where(place == lane, 1.0, 0.0)
        return jnp.transpose(hot)[: p.group_slots].astype(jnp.bfloat16)

    for mask in range(2 ** (steps - 1), 2**steps):
        for i in range(len(sources)):
            flights[i, mask].wait_recv()
    for c in loads:
        c.wait()

    tile_rows = min(256, p.chunk_toks)
    tile_cols = min(256, p.hidden)

    def forward(c):
        @pl.loop(0, p.chunk_toks // tile_rows)
        def _(t):
            first_row = pl.multiple_of(c * p.chunk_toks + t * tile_rows, tile_rows)
            rows = pl.ds(first_row, tile_rows)
            w = weights[rows, :][:, :1]
            scaled[...] = (all_cot[rows, :].astype(jnp.float32) * w).astype(jnp.bfloat16)

            @pl.loop(0, p.hidden // tile_cols)
            def _(u):
                cols = pl.ds(pl.multiple_of(u * tile_cols, tile_cols), tile_cols)
                x = all_tok[rows, :]
                gate = jnp.dot(x, w_gate[0, :, cols], preferred_element_type=jnp.float32)
                upper = jnp.dot(x, w_up[0, :, cols], preferred_element_type=jnp.float32)
                back = jnp.dot(
                    scaled[...], w_down[0, :, cols], preferred_element_type=jnp.float32
                )
                sig = jax.nn.sigmoid(gate)
                backs[0, rows, cols] = (
                    back * upper * sig * (1.0 + gate * (1.0 - sig))
                ).astype(jnp.bfloat16)
                backs[1, rows, cols] = (back * gate * sig).astype(jnp.bfloat16)
                backs[2, rows, cols] = (gate * sig * upper).astype(jnp.bfloat16)

    def pack(c):
        for gl in range(p.chunk_groups):
            g = c * p.chunk_groups + gl
            pick = picker(places, g)
            rows = slice(g * p.group_toks, (g + 1) * p.group_toks)
            kinds = [
                jnp.dot(pick, backs[k, rows, :], preferred_element_type=jnp.float32).astype(
                    jnp.bfloat16
                )
                for k in range(KINDS)
            ]
            spare = p.group_rows - KINDS * p.group_slots
            if spare:
                kinds.append(jnp.zeros((spare, p.hidden), jnp.bfloat16))
            whole = jnp.concatenate(kinds, axis=0)
            for t in range(p.col_tiles):
                j = (gl * p.col_tiles + t) * p.row_split
                piece = whole[:, t * LANES : (t + 1) * LANES]
                packed[c, j : j + p.row_split] = piece.reshape(
                    p.row_split, p.piece_rows, LANES
                )

    def spread(c, o):
        to_h = (h + o) % half
        return pltpu.make_async_remote_copy(
            src_ref=packed.at[c, to_h],
            dst_ref=arrived[c].at[h],
            send_sem=send1.at[c, o],
            recv_sem=recv1.at[c, o],
            device_id=(d, base + to_h),
            device_id_type=MESH,
        )

    def swap(c):
        return pltpu.make_async_remote_copy(
            src_ref=staged[c],
            dst_ref=swapped[c],
            send_sem=send2.at[c],
            recv_sem=recv2.at[c],
            device_id=mirror,
            device_id_type=MESH,
        )

    def collect(c, o):
        to_h = (h + o) % half
        return pltpu.make_async_remote_copy(
            src_ref=ordered[c].at[to_h],
            dst_ref=landed.at[c, h],
            send_sem=send3.at[c, o],
            recv_sem=recv3.at[c, o],
            device_id=(d, base + to_h),
            device_id_type=MESH,
        )

    def stay_first(c):
        return pltpu.make_async_copy(packed.at[c, h], arrived[c].at[h], stay1.at[c])

    def stay_last(c):
        return pltpu.make_async_copy(ordered[c].at[h], landed.at[c, h], stay3.at[c])

    def begin(c):
        forward(c)
        pack(c)
        stay_first(c).start()

        @pl.loop(1, half)
        def _(o):
            spread(c, o).start()

    def cross_list(start):
        flags, before, count = [], [], 0
        for i in range(half):
            m = match[start + i]
            inside = (m >= start) & (m < start + half)
            flag = jnp.where(inside, 0, 1)
            flags.append(flag)
            before.append(count)
            count = count + flag
        return flags, before

    def cross_at(listed, k):
        flags, before = listed
        found = 0
        for i in range(half):
            found = found + jnp.where((flags[i] == 1) & (before[i] == k), i, 0)
        return found

    other = (base + half) % n
    full = crossing == half

    def swap_on(c):
        stay_first(c).wait()

        @pl.loop(1, half)
        def _(o):
            spread(c, o).wait_recv()

        if full:
            staged[c][...] = arrived[c][...]
        else:
            mine = cross_list(base)
            for k in range(crossing):
                staged[c][k] = arrived[c][cross_at(mine, k)]
        swap(c).start()

    def collect_on(c):
        swap(c).wait_recv()
        theirs = None if full else cross_list(other)
        for i in range(half):
            m = match[base + i]
            inside = (m >= base) & (m < base + half)
            near = arrived[c][jnp.where(inside, m - base, 0)]
            if full:
                far_at = jnp.where(inside, 0, m - other)
            else:
                far_at = 0
                for k in range(half):
                    far_at = far_at + jnp.where(m - other == k, theirs[1][k], 0)
                far_at = jnp.where(inside, 0, far_at)
            far = swapped[c][far_at]
            ordered[c][i] = jnp.where(inside, near, far)
        stay_last(c).start()

        @pl.loop(1, half)
        def _(o):
            collect(c, o).start()

    r_orders = reduce_orders(p.expert_bits, p.dp_bits)
    r_flights = [[], []]

    def split(i, s):
        axis, bit = r_orders[i][s]
        if s == 0:
            ref, rows = part, pl.ds(i * rows_half, rows_half)
        else:
            ref, rows = sums[i][s - 1], slice(None)
        left = [b for a, b in r_orders[i][s:] if a == "expert"]
        left = sorted(left, reverse=True)
        if axis == "expert":
            mine = (e // 2**bit) % 2
            spot = left.index(bit)

            def where(v):
                return tuple(
                    [slice(None)] * spot + [v] + [slice(None)] * (len(left) - spot - 1)
                ) + (rows, slice(None))

            return ref, where(mine), where(1 - mine)
        mine = (d // 2**bit) % 2
        span = 2**bit * width
        head = (slice(None),) * len(left) + (rows,)
        keep = head + (pl.ds(pl.multiple_of(mine * span, LANES), span),)
        give = head + (pl.ds(pl.multiple_of((1 - mine) * span, LANES), span),)
        return ref, keep, give

    def start_step(i, s):
        ref, _, give = split(i, s)
        c = pltpu.make_async_remote_copy(
            src_ref=ref.at[give],
            dst_ref=came[i][s],
            send_sem=rsend.at[i, s],
            recv_sem=rrecv.at[i, s],
            device_id=peer(*r_orders[i][s]),
            device_id_type=MESH,
        )
        c.start()
        r_flights[i].append(c)

    def end_step(i, s):
        ref, keep, _ = split(i, s)
        r_flights[i][s].wait_recv()
        total = ref[keep].astype(jnp.float32) + came[i][s][...].astype(jnp.float32)
        sums[i][s][...] = total.astype(sums[i][s].dtype)

    def next_step(s):
        for i in range(halves):
            end_step(i, s)
            if s + 1 < steps:
                start_step(i, s + 1)

    def pack_rows(src, dst, w_ref):
        for g in range(p.groups):
            pick = picker(p_places, g)
            rows = slice(g * p.group_toks, (g + 1) * p.group_toks)
            at_rows = slice(g * p.group_slots, (g + 1) * p.group_slots)
            span = min(512, p.model)
            for t in range(0, p.model, span):
                x = src[rows, t : t + span]
                if w_ref is not None:
                    x = (x.astype(jnp.float32) * w_ref[rows, :][:, :1]).astype(jnp.bfloat16)
                dst[at_rows, t : t + span] = jnp.dot(
                    pick, x, preferred_element_type=jnp.float32
                ).astype(jnp.bfloat16)

    for c in range(chunks):
        begin(c)
    swap_on(0)
    tile = min(512, p.model)
    for t in range(0, p.model, tile):
        piece = lax.dot_general(
            backs[0], w_gate[0, t : t + tile], contract_cols, preferred_element_type=jnp.float32
        )
        piece += lax.dot_general(
            backs[1], w_up[0, t : t + tile], contract_cols, preferred_element_type=jnp.float32
        )
        shape = part.shape[:-1] + (tile,)
        part[..., t : t + tile] = piece.astype(part.dtype).reshape(shape)
    for i in range(halves):
        start_step(i, 0)
    for c in range(1, chunks):
        swap_on(c)
    pack_rows(all_tok, x_rows, None)
    row_out = pltpu.make_async_copy(x_rows, out_rows, osem.at[0])
    row_out.start()
    next_step(0)
    pack_rows(all_cot, x_grads, p_weights)
    grad_out = pltpu.make_async_copy(x_grads, out_grads, osem.at[1])
    grad_out.start()
    next_step(1)
    collect_on(0)
    for s in range(2, steps - 1):
        next_step(s)
    for c in range(1, chunks):
        collect_on(c)
    next_step(steps - 1)
    for i in range(halves):
        summed[pl.ds(i * rows_half, rows_half), :] = sums[i][steps - 1][...]
    result_out = pltpu.make_async_copy(summed, result, osem.at[2])
    result_out.start()

    for c in flights.values():
        c.wait_send()
    for c in meta_flights.values():
        c.wait_send()
    for f in r_flights:
        for c in f:
            c.wait_send()
    row_out.wait()
    grad_out.wait()
    result_out.wait()
    for c in range(chunks):
        stay_last(c).wait()
        swap(c).wait_send()

        @pl.loop(1, half)
        def _(o):
            spread(c, o).wait_send()
            collect(c, o).wait_send()
            collect(c, o).wait_recv()


def communicate(p, crossing, call_id, operands):
    dtype = operands[1].dtype
    reduce_buffers = []
    for order in reduce_orders(p.expert_bits, p.dp_bits):
        for shape in reduce_shapes(order, p.expert_bits, p.dp_bits, p.tok_rows // 2, p.width):
            reduce_buffers.append(pltpu.VMEM(shape, dtype))
    piece = (p.piece_rows, LANES)
    weight = operands[-1].shape
    dma = pltpu.SemaphoreType.DMA
    steps, chunks, half = p.steps, p.chunks, p.half
    scratch = (
        reduce_buffers
        + reduce_buffers
        + [pltpu.VMEM((half,) + piece, dtype)] * chunks
        + [pltpu.VMEM((crossing,) + piece, dtype)] * (2 * chunks)
        + [pltpu.VMEM((half,) + piece, dtype)] * chunks
        + [
            pltpu.VMEM((p.total, p.model), dtype),
            pltpu.VMEM((p.total, p.model), dtype),
            pltpu.VMEM((p.n_expert, p.top_count, p.tok_rows), jnp.int32),
            pltpu.VMEM((p.n_expert, p.top_count, p.tok_rows), jnp.float32),
            pltpu.VMEM(weight, dtype),
            pltpu.VMEM(weight, dtype),
            pltpu.VMEM(weight, dtype),
            pltpu.VMEM((p.total, LANES), jnp.float32),
            pltpu.VMEM((p.total, LANES), jnp.float32),
            pltpu.VMEM((p.total, LANES), jnp.float32),
            pltpu.VMEM((p.total, LANES), jnp.float32),
            pltpu.VMEM((min(256, p.chunk_toks), p.model), dtype),
            pltpu.VMEM((KINDS, p.total, p.hidden), dtype),
            pltpu.VMEM((chunks, half) + piece, dtype),
            pltpu.VMEM((2,) * p.expert_bits + (p.tok_rows, p.model), dtype),
            pltpu.VMEM((p.slots, p.model), dtype),
            pltpu.VMEM((p.slots, p.model), dtype),
            pltpu.VMEM((p.tok_rows, p.width), dtype),
            dma((2 * p.row_parts, 2**steps)),
            dma((2 * p.row_parts, 2**steps)),
            dma((2, p.n_expert)),
            dma((2, p.n_expert)),
            dma((4,)),
            dma((3,)),
            dma((chunks, half)),
            dma((chunks, half)),
            dma((chunks,)),
            dma((chunks,)),
            dma((chunks, half)),
            dma((chunks, half)),
            dma((chunks,)),
            dma((chunks,)),
            dma((2, steps)),
            dma((2, steps)),
            dma((3,)),
        ]
    )
    anywhere = pl.BlockSpec(memory_space=pl.ANY)
    return pl.pallas_call(
        functools.partial(comm_kernel, p, crossing),
        out_shape=(
            jax.ShapeDtypeStruct((chunks, half) + piece, dtype),
            jax.ShapeDtypeStruct((p.slots, p.model), dtype),
            jax.ShapeDtypeStruct((p.slots, p.model), dtype),
            jax.ShapeDtypeStruct((p.tok_rows, p.width), dtype),
        ),
        in_specs=[pl.BlockSpec(memory_space=pltpu.SMEM)] + [anywhere] * 7,
        out_specs=[anywhere] * 4,
        scratch_shapes=scratch,
        compiler_params=pltpu.CompilerParams(
            collective_id=call_id, has_side_effects=True, vmem_limit_bytes=64 * 2**20 - 2**16
        ),
    )(*operands)


def final_kernel(p, landed, rows, grads, summed, g_gate, g_up, g_down, out, acts):
    @pl.when(pl.program_id(0) == 0)
    def _():
        out[...] = summed[...]
        for c in range(p.chunks):
            for gl in range(p.chunk_groups):
                at = (c * p.chunk_groups + gl) * p.group_slots
                for t in range(p.col_tiles):
                    j = (gl * p.col_tiles + t) * p.row_split
                    piece = landed[c, j : j + p.row_split].reshape(p.group_rows, LANES)
                    for k in range(KINDS):
                        acts[k, at : at + p.group_slots, t * LANES : (t + 1) * LANES] = piece[
                            k * p.group_slots : (k + 1) * p.group_slots
                        ]

    x = rows[...]
    g_gate[0] = lax.dot_general(x, acts[0], contract_rows, preferred_element_type=jnp.float32)
    g_up[0] = lax.dot_general(x, acts[1], contract_rows, preferred_element_type=jnp.float32)
    g_down[0] = lax.dot_general(
        grads[...], acts[2], contract_rows, preferred_element_type=jnp.float32
    )


def finish(p, landed, rows, grads, summed):
    tile = min(256, p.model)
    wide = pl.BlockSpec((p.slots, tile), lambda i: (0, i))
    grad = pl.BlockSpec((1, tile, p.hidden), lambda i: (0, i, 0))
    grad_shape = jax.ShapeDtypeStruct((1, p.model, p.hidden), jnp.float32)
    whole = pl.BlockSpec(landed.shape, lambda i: (0, 0, 0, 0))
    small = pl.BlockSpec(summed.shape, lambda i: (0, 0))
    return pl.pallas_call(
        functools.partial(final_kernel, p),
        out_shape=(
            grad_shape,
            grad_shape,
            grad_shape,
            jax.ShapeDtypeStruct(summed.shape, summed.dtype),
        ),
        grid=(p.model // tile,),
        in_specs=[whole, wide, wide, small],
        out_specs=[grad, grad, grad, small],
        scratch_shapes=[pltpu.VMEM((KINDS, p.slots, p.hidden), landed.dtype)],
    )(landed, rows, grads, summed)


def local(n_expert, n_dp, tokens, cotangent, routes, probs, matching, w_gate, w_up, w_down):
    tok_rows, top_count = routes.shape
    p = Plan(n_expert, n_dp, tok_rows, tokens.shape[1], top_count, w_gate.shape[2])
    operands = (matching, tokens, cotangent, routes.T, probs.T, w_gate, w_up, w_down)
    sizes = (p.half // 2, 3 * p.half // 4, p.half)
    pairs = jnp.sum((matching[: p.half] >= p.half).astype(jnp.int32))
    which = sum((pairs > size).astype(jnp.int32) for size in sizes[:-1])
    calls = [
        functools.partial(lambda size, i, *a: communicate(p, size, i, a), size, i)
        for i, size in enumerate(sizes)
    ]
    landed, rows, grads, summed = lax.switch(which, calls, *operands)
    g_gate, g_up, g_down, input_grad = finish(p, landed, rows, grads, summed)
    return input_grad, g_gate, g_up, g_down


def solution(mesh):
    weights = P("expert", None, "dp")
    return jax.shard_map(
        functools.partial(local, mesh.shape["expert"], mesh.shape["dp"]),
        mesh=mesh,
        in_specs=(
            P("expert", "dp"),
            P("expert", "dp"),
            P("expert", None),
            P("expert", None),
            P(),
            weights,
            weights,
            weights,
        ),
        out_specs=(P("expert", "dp"), weights, weights, weights),
        check_vma=False,
    )
```

```python
import functools
import math

import jax
import jax.numpy as jnp
from jax import lax
from jax.experimental import pallas as pl
from jax.experimental.pallas import tpu as pltpu
from jax.sharding import PartitionSpec as P

contract_cols = (((1,), (1,)), ((), ()))
MESH = pl.DeviceIdType.MESH
KINDS = 3
LANES = 128


def bit_count(size):
    return size.bit_length() - 1


def gather_orders(expert_bits, dp_bits):
    far = [("expert", b) for b in range(expert_bits - 1, 1, -1)]
    mid = [("expert", 1)]
    last = [("expert", 0)]
    across = [("dp", b) for b in range(dp_bits)]
    return (
        far + across + mid + last,
        across + far + mid + last,
        far + mid + across + last,
        mid + far + across + last,
        far + mid + last,
    )


def landing_order(steps, parts):
    def turn(mask):
        top = 2 ** (mask.bit_length() - 1)
        return (mask - top, top)

    return [(i, mask) for mask in sorted(range(1, 2 ** (steps - 1)), key=turn) for i in range(parts)]


def reduce_orders(expert_bits, dp_bits):
    far = [("expert", b) for b in range(2, expert_bits)]
    mid = [("expert", 1)]
    near = [("expert", 0)]
    across = [("dp", b) for b in range(dp_bits - 1, -1, -1)]
    return (near + across + mid + far, near + mid + across + far)


def reduce_shapes(order, expert_bits, dp_bits, rows, width):
    left_e, left_d = expert_bits, dp_bits
    shapes = []
    for axis, _ in order:
        if axis == "expert":
            left_e -= 1
        else:
            left_d -= 1
        shapes.append((2,) * left_e + (rows, width * 2**left_d))
    return shapes


class Plan:
    def __init__(self, n_expert, n_dp, tok_rows, width, top_count, hidden):
        self.n_expert, self.n_dp = n_expert, n_dp
        self.expert_bits, self.dp_bits = bit_count(n_expert), bit_count(n_dp)
        self.tok_rows, self.width, self.hidden = tok_rows, width, hidden
        self.top_count = top_count
        self.model = width * n_dp
        self.total = n_expert * tok_rows
        self.capacity = max(2, 5 * tok_rows * top_count // (4 * n_expert))
        self.blocks = 16 // math.gcd(16, self.capacity)
        self.groups = n_expert // self.blocks
        self.group_slots = self.blocks * self.capacity
        self.group_toks = self.blocks * tok_rows
        self.slots = self.groups * self.group_slots
        self.half = n_expert // 2
        self.span = min(256, hidden)
        self.spans = hidden // self.span
        self.chunks = KINDS * self.spans
        self.col_tiles = self.span // LANES
        self.row_split = self.half // self.col_tiles
        unit = 16 * self.row_split
        self.padded = -(-self.slots // unit) * unit
        self.piece_rows = self.padded // self.row_split
        self.row_tile = min(256, self.total)
        self.steps = self.expert_bits + self.dp_bits
        self.row_parts = 2 if 2**self.steps <= 128 else 1


def comm_kernel(
    p,
    crossing,
    match,
    tokens,
    cotangent,
    routes,
    probs,
    h_gate,
    h_up,
    h_down,
    landed,
    out_rows,
    out_grads,
    result,
    *scratch,
):
    n, half = p.n_expert, p.half
    steps, chunks = p.steps, p.chunks
    halves = 2
    sums = [scratch[i * steps : (i + 1) * steps] for i in range(halves)]
    came = [scratch[(halves + i) * steps : (halves + i + 1) * steps] for i in range(halves)]
    rest = scratch[2 * halves * steps :]
    arrived = rest[:chunks]
    swapped = rest[chunks : 2 * chunks]
    staged = rest[2 * chunks : 3 * chunks]
    ordered = rest[3 * chunks : 4 * chunks]
    (
        all_tok,
        all_cot,
        all_routes,
        all_probs,
        w_gate,
        w_up,
        w_down,
        weights,
        p_weights,
        picks,
        p_picks,
        gates,
        uppers,
        backs,
        packed,
        index,
        part,
        x_rows,
        x_cols,
        g_cols,
        summed,
        gsend,
        grecv,
        msend,
        mrecv,
        own,
        wsem,
        send1,
        recv1,
        send2,
        recv2,
        send3,
        recv3,
        stay1,
        stay3,
        rsend,
        rrecv,
        osem,
    ) = rest[4 * chunks :]
    e = lax.axis_index("expert")
    d = lax.axis_index("dp")
    h = e % half
    base = e - h
    step_of = [2**b * (1 - 2 * ((e // 2**b) % 2)) for b in range(p.expert_bits)]
    step_dp = [2**b * (1 - 2 * ((d // 2**b) % 2)) for b in range(p.dp_bits)]
    rows_half = p.tok_rows // 2
    part_rows = p.tok_rows // p.row_parts
    width = p.width

    def peer(axis, bit):
        if axis == "expert":
            return (d, e + step_of[bit])
        return (d + step_dp[bit], e)

    def origin(order, mask):
        at_e, at_d = e, d
        for k, (axis, bit) in enumerate(order):
            if mask >> k & 1:
                if axis == "expert":
                    at_e = at_e + step_of[bit]
                else:
                    at_d = at_d + step_dp[bit]
        return at_e, at_d

    orders = gather_orders(p.expert_bits, p.dp_bits)
    sources = (
        (tokens, all_tok, 0, orders[0]),
        (cotangent, all_cot, 0, orders[1]),
        (tokens, all_tok, 1, orders[2]),
        (cotangent, all_cot, 1, orders[3]),
    )[: 2 * p.row_parts]

    def block(dst, index, at_e, at_d):
        row = pl.multiple_of(at_e * p.tok_rows + index * part_rows, part_rows)
        col = pl.multiple_of(at_d * width, width)
        return dst.at[pl.ds(row, part_rows), pl.ds(col, width)]

    metas = ((routes, all_routes), (probs, all_probs))
    locals_ = []
    for i, (src, dst) in enumerate(((tokens, all_tok), (cotangent, all_cot))):
        row = pl.multiple_of(e * p.tok_rows, p.tok_rows)
        col = pl.multiple_of(d * width, width)
        c = pltpu.make_async_copy(
            src, dst.at[pl.ds(row, p.tok_rows), pl.ds(col, width)], own.at[i]
        )
        c.start()
        locals_.append(c)
    for i, (src, dst) in enumerate(metas):
        c = pltpu.make_async_copy(src, dst.at[e], own.at[2 + i])
        c.start()
        locals_.append(c)

    barrier = pltpu.get_barrier_semaphore()

    @pl.loop(1, half)
    def _(o):
        pl.semaphore_signal(
            barrier, inc=1, device_id=(d, base + (h + o) % half), device_id_type=MESH
        )

    mirror = (d, (e + half) % n)
    pl.semaphore_signal(barrier, inc=1, device_id=mirror, device_id_type=MESH)
    for b in range(p.dp_bits):
        pl.semaphore_signal(barrier, inc=1, device_id=(d + step_dp[b], e), device_id_type=MESH)
    other = (base + half) % n
    full = crossing == half

    def cross_list(start):
        flags, counts, count = [], [], 0
        for i in range(half):
            m = match[start + i]
            flag = jnp.where((m >= start) & (m < start + half), 0, 1)
            flags.append(flag)
            counts.append(count)
            count = count + flag
        return flags, counts

    if not full:
        mine, theirs = cross_list(base), cross_list(other)
    for k in range(half):
        found = k
        if not full:
            found = 0
            for i in range(half):
                found = found + jnp.where((mine[0][i] == 1) & (mine[1][i] == k), i, 0)
        m = match[base + k]
        inside = (m >= base) & (m < base + half)
        far = m - other
        if not full:
            far = 0
            for i in range(half):
                far = far + jnp.where(m - other == i, theirs[1][i], 0)
        index[0, k] = found
        index[1, k] = jnp.where(inside, m - base, 0)
        index[2, k] = jnp.where(inside, 0, far)
        index[3, k] = jnp.where(inside, 1, 0)

    pl.semaphore_wait(barrier, half + p.dp_bits)

    def flight(i, mask, k):
        src, dst, index, order = sources[i]
        at = block(dst, index, *origin(order, mask))
        if mask == 0:
            src = src.at[pl.ds(index * part_rows, part_rows)]
        else:
            src = at
        got = mask + 2**k
        return pltpu.make_async_remote_copy(
            src_ref=src,
            dst_ref=at,
            send_sem=gsend.at[i, got],
            recv_sem=grecv.at[i, got],
            device_id=peer(*order[k]),
            device_id_type=MESH,
        )

    def meta_flight(i, mask, k):
        src, dst = metas[i]
        at = dst.at[origin(orders[4], mask)[0]]
        got = mask + 2**k
        return pltpu.make_async_remote_copy(
            src_ref=src if mask == 0 else at,
            dst_ref=at,
            send_sem=msend.at[i, got],
            recv_sem=mrecv.at[i, got],
            device_id=peer(*orders[4][k]),
            device_id_type=MESH,
        )

    flights, meta_flights = {}, {}

    def send_on(i, mask):
        top = mask.bit_length()
        for k in range(top, steps):
            c = flight(i, mask, k)
            c.start()
            flights[i, mask + 2**k] = c

    def meta_on(i, mask):
        for k in range(mask.bit_length(), p.expert_bits):
            c = meta_flight(i, mask, k)
            c.start()
            meta_flights[i, mask + 2**k] = c

    for i in range(len(sources)):
        send_on(i, 0)
    for i in range(len(metas)):
        meta_on(i, 0)
    loads = []
    for i, (src, dst) in enumerate(((h_gate, w_gate), (h_up, w_up), (h_down, w_down))):
        c = pltpu.make_async_copy(src, dst, wsem.at[i])
        c.start()
        loads.append(c)

    meta_masks = list(range(1, 2**p.expert_bits))
    for count, (i, mask) in enumerate(landing_order(steps, len(sources))):
        flights[i, mask].wait_recv()
        send_on(i, mask)
        if count % len(sources) == len(sources) - 1 and meta_masks:
            meta = meta_masks.pop(0)
            for k in range(len(metas)):
                meta_flights[k, meta].wait_recv()
                meta_on(k, meta)
    for meta in meta_masks:
        for k in range(len(metas)):
            meta_flights[k, meta].wait_recv()
            meta_on(k, meta)
    for c in locals_:
        c.wait()

    partner = match[e]
    tok = p.tok_rows
    at = lax.broadcasted_iota(jnp.int32, (tok, tok), 0)
    to = lax.broadcasted_iota(jnp.int32, (tok, tok), 1)
    before = jnp.where(at < to, 1.0, 0.0).astype(jnp.bfloat16)
    start = (lax.broadcasted_iota(jnp.int32, (n, tok), 0) % p.blocks) * p.capacity
    tables = []
    for who in (e, partner):
        hit = all_routes[...] == who
        w = jnp.sum(jnp.where(hit, all_probs[...], 0.0), axis=1)
        f = jnp.sum(jnp.where(hit, 1.0, 0.0), axis=1)
        rank = jnp.dot(f.astype(jnp.bfloat16), before, preferred_element_type=jnp.float32)
        place = jnp.where(f > 0.5, rank + start.astype(jnp.float32), -1.0)
        tables.append((jnp.transpose(w), jnp.transpose(place)))
    for (w, place), w_ref, pick_ref in (
        (tables[0], weights, picks),
        (tables[1], p_weights, p_picks),
    ):
        for g in range(p.groups):
            cols = []
            for b in range(g * p.blocks, (g + 1) * p.blocks):
                w_ref[b * tok : (b + 1) * tok, :] = jnp.broadcast_to(w[:, b : b + 1], (tok, LANES))
                cols.append(jnp.broadcast_to(place[:, b : b + 1], (tok, LANES)))
            spots = jnp.concatenate(cols, axis=0)
            lane = lax.broadcasted_iota(jnp.int32, spots.shape, 1).astype(jnp.float32)
            hot = jnp.transpose(jnp.where(spots == lane, 1.0, 0.0))
            pick_ref[g] = hot[: p.group_slots].astype(jnp.bfloat16)

    for mask in range(2 ** (steps - 1), 2**steps):
        for i in range(len(sources)):
            flights[i, mask].wait_recv()
    for c in loads:
        c.wait()

    tiles = p.total // p.row_tile
    tile_bits = bit_count(tiles)

    def tile_of(t):
        return tuple((t >> (tile_bits - 1 - i)) & 1 for i in range(tile_bits))

    def scale():
        for t in range(tiles):
            rows = slice(t * p.row_tile, (t + 1) * p.row_tile)
            value = (all_cot[rows, :].astype(jnp.float32) * weights[rows, :][:, :1]).astype(
                jnp.bfloat16
            )
            shape = part.shape[tile_bits:]
            part[tile_of(t)] = value.reshape(shape)

    def first_half(u):
        cols = slice(u * p.span, (u + 1) * p.span)
        for t in range(tiles):
            rows = slice(t * p.row_tile, (t + 1) * p.row_tile)
            x = all_tok[rows, :]
            gate = jnp.dot(x, w_gate[0, :, cols], preferred_element_type=jnp.float32)
            upper = jnp.dot(x, w_up[0, :, cols], preferred_element_type=jnp.float32)
            gates[rows, :] = gate
            uppers[rows, :] = upper
            backs[2, rows, cols] = (gate * jax.nn.sigmoid(gate) * upper).astype(jnp.bfloat16)

    def second_half(u):
        cols = slice(u * p.span, (u + 1) * p.span)
        for t in range(tiles):
            rows = slice(t * p.row_tile, (t + 1) * p.row_tile)
            grads = part[tile_of(t)].reshape(p.row_tile, p.model)
            back = jnp.dot(grads, w_down[0, :, cols], preferred_element_type=jnp.float32)
            gate = gates[rows, :]
            sig = jax.nn.sigmoid(gate)
            backs[0, rows, cols] = (
                back * uppers[rows, :] * sig * (1.0 + gate * (1.0 - sig))
            ).astype(jnp.bfloat16)
            backs[1, rows, cols] = (back * gate * sig).astype(jnp.bfloat16)

    def pack(c, kind, u):
        per = p.group_slots // p.piece_rows
        for g in range(p.groups):
            rows = slice(g * p.group_toks, (g + 1) * p.group_toks)
            value = backs[kind, rows, u * p.span : (u + 1) * p.span]
            value = jnp.dot(picks[g], value, preferred_element_type=jnp.float32)
            value = value.astype(jnp.bfloat16)
            for t in range(p.col_tiles):
                j = t * p.row_split + g * per
                packed[c, j : j + per] = value[:, t * LANES : (t + 1) * LANES].reshape(
                    per, p.piece_rows, LANES
                )
        spare = p.row_split - p.groups * per
        if spare:
            for t in range(p.col_tiles):
                j = (t + 1) * p.row_split
                packed[c, j - spare : j] = jnp.zeros((spare, p.piece_rows, LANES), jnp.bfloat16)

    def spread(c, o):
        to_h = (h + o) % half
        return pltpu.make_async_remote_copy(
            src_ref=packed.at[c, to_h],
            dst_ref=arrived[c].at[h],
            send_sem=send1.at[c, o],
            recv_sem=recv1.at[c, o],
            device_id=(d, base + to_h),
            device_id_type=MESH,
        )

    def swap(c):
        return pltpu.make_async_remote_copy(
            src_ref=staged[c],
            dst_ref=swapped[c],
            send_sem=send2.at[c],
            recv_sem=recv2.at[c],
            device_id=mirror,
            device_id_type=MESH,
        )

    def collect(c, o):
        to_h = (h + o) % half
        return pltpu.make_async_remote_copy(
            src_ref=ordered[c].at[to_h],
            dst_ref=landed.at[c, h],
            send_sem=send3.at[c, o],
            recv_sem=recv3.at[c, o],
            device_id=(d, base + to_h),
            device_id_type=MESH,
        )

    def stay_first(c):
        return pltpu.make_async_copy(packed.at[c, h], arrived[c].at[h], stay1.at[c])

    def stay_last(c):
        return pltpu.make_async_copy(ordered[c].at[h], landed.at[c, h], stay3.at[c])

    def begin(c, kind, u):
        pack(c, kind, u)
        stay_first(c).start()

        @pl.loop(1, half)
        def _(o):
            spread(c, o).start()

    def swap_on(c):
        stay_first(c).wait()

        @pl.loop(1, half)
        def _(o):
            spread(c, o).wait_recv()

        if full:
            staged[c][...] = arrived[c][...]
        else:
            for k in range(crossing):
                staged[c][k] = arrived[c][index[0, k]]
        swap(c).start()

    def collect_on(c):
        swap(c).wait_recv()
        for i in range(half):
            near = arrived[c][index[1, i]]
            far = swapped[c][index[2, i]]
            ordered[c][i] = jnp.where(index[3, i] == 1, near, far)
        stay_last(c).start()

        @pl.loop(1, half)
        def _(o):
            collect(c, o).start()

    r_orders = reduce_orders(p.expert_bits, p.dp_bits)
    r_flights = [[], []]

    def split(i, s):
        axis, bit = r_orders[i][s]
        if s == 0:
            ref, rows = part, pl.ds(i * rows_half, rows_half)
        else:
            ref, rows = sums[i][s - 1], slice(None)
        left = [b for a, b in r_orders[i][s:] if a == "expert"]
        left = sorted(left, reverse=True)
        if axis == "expert":
            mine = (e // 2**bit) % 2
            spot = left.index(bit)

            def where(v):
                return tuple(
                    [slice(None)] * spot + [v] + [slice(None)] * (len(left) - spot - 1)
                ) + (rows, slice(None))

            return ref, where(mine), where(1 - mine)
        mine = (d // 2**bit) % 2
        span = 2**bit * width
        head = (slice(None),) * len(left) + (rows,)
        keep = head + (pl.ds(pl.multiple_of(mine * span, LANES), span),)
        give = head + (pl.ds(pl.multiple_of((1 - mine) * span, LANES), span),)
        return ref, keep, give

    def start_step(i, s):
        ref, _, give = split(i, s)
        c = pltpu.make_async_remote_copy(
            src_ref=ref.at[give],
            dst_ref=came[i][s],
            send_sem=rsend.at[i, s],
            recv_sem=rrecv.at[i, s],
            device_id=peer(*r_orders[i][s]),
            device_id_type=MESH,
        )
        c.start()
        r_flights[i].append(c)

    def end_step(i, s):
        ref, keep, _ = split(i, s)
        r_flights[i][s].wait_recv()
        total = ref[keep].astype(jnp.float32) + came[i][s][...].astype(jnp.float32)
        sums[i][s][...] = total.astype(sums[i][s].dtype)

    def next_step(s):
        for i in range(halves):
            end_step(i, s)
            if s + 1 < steps:
                start_step(i, s + 1)

    def pack_rows(src, dst, w_ref):
        span = min(512, p.model)

        @pl.loop(0, p.model // span)
        def _(t):
            cols = pl.ds(pl.multiple_of(t * span, span), span)
            for g in range(p.groups):
                rows = slice(g * p.group_toks, (g + 1) * p.group_toks)
                at_rows = slice(g * p.group_slots, (g + 1) * p.group_slots)
                x = src[rows, cols]
                if w_ref is not None:
                    x = (x.astype(jnp.float32) * w_ref[rows, :][:, :1]).astype(jnp.bfloat16)
                x_rows[at_rows, :] = jnp.dot(
                    p_picks[g], x, preferred_element_type=jnp.float32
                ).astype(jnp.bfloat16)
            dst[cols, :] = jnp.transpose(x_rows[...])

    def make_part(first, last):
        tile = min(512, p.model)

        @pl.loop(first * p.model // (2 * tile), last * p.model // (2 * tile))
        def _(t):
            cols = pl.ds(pl.multiple_of(t * tile, tile), tile)
            piece = lax.dot_general(
                backs[0], w_gate[0, cols, :], contract_cols, preferred_element_type=jnp.float32
            )
            piece += lax.dot_general(
                backs[1], w_up[0, cols, :], contract_cols, preferred_element_type=jnp.float32
            )
            shape = part.shape[:-1] + (tile,)
            part[..., cols] = piece.astype(part.dtype).reshape(shape)

    for u in range(p.spans):
        first_half(u)
        begin(KINDS * u, 2, u)
        if u == 0:
            scale()
        second_half(u)
        begin(KINDS * u + 1, 0, u)
        begin(KINDS * u + 2, 1, u)
    make_part(0, 1)
    swap_on(0)
    make_part(1, 2)
    for i in range(halves):
        start_step(i, 0)
    for c in range(1, KINDS):
        swap_on(c)
    next_step(0)
    for c in range(KINDS, chunks):
        swap_on(c)
    pack_rows(all_tok, x_cols, None)
    row_out = pltpu.make_async_copy(x_cols, out_rows, osem.at[0])
    row_out.start()
    pace = 42 * crossing / (half * chunks)
    events = [(10 + pace * (c + 1), 0, c) for c in range(chunks)]
    events += [(13.5 + 5.5 * s, 1, s) for s in range(1, steps)]
    events.append((10 + 1.1 * pace, 2, 0))
    for _, kind, which in sorted(events):
        if kind == 0:
            collect_on(which)
        elif kind == 1:
            next_step(which)
        else:
            pack_rows(all_cot, g_cols, p_weights)
            grad_out = pltpu.make_async_copy(g_cols, out_grads, osem.at[1])
            grad_out.start()
    for i in range(halves):
        summed[pl.ds(i * rows_half, rows_half), :] = sums[i][steps - 1][...]
    result_out = pltpu.make_async_copy(summed, result, osem.at[2])
    result_out.start()

    for c in flights.values():
        c.wait_send()
    for c in meta_flights.values():
        c.wait_send()
    for f in r_flights:
        for c in f:
            c.wait_send()
    row_out.wait()
    grad_out.wait()
    result_out.wait()
    for c in range(chunks):
        stay_last(c).wait()
        swap(c).wait_send()

        @pl.loop(1, half)
        def _(o):
            spread(c, o).wait_send()
            collect(c, o).wait_send()
            collect(c, o).wait_recv()


def communicate(p, crossing, call_id, operands):
    dtype = operands[1].dtype
    reduce_buffers = []
    for order in reduce_orders(p.expert_bits, p.dp_bits):
        for shape in reduce_shapes(order, p.expert_bits, p.dp_bits, p.tok_rows // 2, p.width):
            reduce_buffers.append(pltpu.VMEM(shape, dtype))
    piece = (p.piece_rows, LANES)
    weight = operands[-1].shape
    dma = pltpu.SemaphoreType.DMA
    steps, chunks, half = p.steps, p.chunks, p.half
    scratch = (
        reduce_buffers
        + reduce_buffers
        + [pltpu.VMEM((half,) + piece, dtype)] * chunks
        + [pltpu.VMEM((crossing,) + piece, dtype)] * (2 * chunks)
        + [pltpu.VMEM((half,) + piece, dtype)] * chunks
        + [
            pltpu.VMEM((p.total, p.model), dtype),
            pltpu.VMEM((p.total, p.model), dtype),
            pltpu.VMEM((p.n_expert, p.top_count, p.tok_rows), jnp.int32),
            pltpu.VMEM((p.n_expert, p.top_count, p.tok_rows), jnp.float32),
            pltpu.VMEM(weight, dtype),
            pltpu.VMEM(weight, dtype),
            pltpu.VMEM(weight, dtype),
            pltpu.VMEM((p.total, LANES), jnp.float32),
            pltpu.VMEM((p.total, LANES), jnp.float32),
            pltpu.VMEM((p.groups, p.group_slots, p.group_toks), dtype),
            pltpu.VMEM((p.groups, p.group_slots, p.group_toks), dtype),
            pltpu.VMEM((p.total, p.span), jnp.float32),
            pltpu.VMEM((p.total, p.span), jnp.float32),
            pltpu.VMEM((KINDS, p.total, p.hidden), dtype),
            pltpu.VMEM((chunks, half) + piece, dtype),
            pltpu.SMEM((4, half), jnp.int32),
            pltpu.VMEM((2,) * p.expert_bits + (p.tok_rows, p.model), dtype),
            pltpu.VMEM((p.slots, min(512, p.model)), dtype),
            pltpu.VMEM((p.model, p.slots), dtype),
            pltpu.VMEM((p.model, p.slots), dtype),
            pltpu.VMEM((p.tok_rows, p.width), dtype),
            dma((2 * p.row_parts, 2**steps)),
            dma((2 * p.row_parts, 2**steps)),
            dma((2, p.n_expert)),
            dma((2, p.n_expert)),
            dma((4,)),
            dma((3,)),
            dma((chunks, half)),
            dma((chunks, half)),
            dma((chunks,)),
            dma((chunks,)),
            dma((chunks, half)),
            dma((chunks, half)),
            dma((chunks,)),
            dma((chunks,)),
            dma((2, steps)),
            dma((2, steps)),
            dma((3,)),
        ]
    )
    anywhere = pl.BlockSpec(memory_space=pl.ANY)
    return pl.pallas_call(
        functools.partial(comm_kernel, p, crossing),
        out_shape=(
            jax.ShapeDtypeStruct((chunks, half) + piece, dtype),
            jax.ShapeDtypeStruct((p.model, p.slots), dtype),
            jax.ShapeDtypeStruct((p.model, p.slots), dtype),
            jax.ShapeDtypeStruct((p.tok_rows, p.width), dtype),
        ),
        in_specs=[pl.BlockSpec(memory_space=pltpu.SMEM)] + [anywhere] * 7,
        out_specs=[anywhere] * 4,
        scratch_shapes=scratch,
        compiler_params=pltpu.CompilerParams(
            collective_id=call_id, has_side_effects=True, vmem_limit_bytes=64 * 2**20 - 2**16
        ),
    )(*operands)


def final_kernel(
    p, landed, rows, grads, summed, g_gate, g_up, g_down, out, items, x, g, small, acts, sums,
    item_sem, x_sem, g_sem, small_sem, out_sem,
):
    tile = min(256, p.model)
    count = p.model // tile
    item_in = pltpu.make_async_copy(landed, items, item_sem)
    item_in.start()

    def load(i):
        at = pl.ds(pl.multiple_of(i * tile, tile), tile)
        return (
            pltpu.make_async_copy(rows.at[at], x.at[at], x_sem.at[i]),
            pltpu.make_async_copy(grads.at[at], g.at[at], g_sem.at[i]),
        )

    def store(i):
        at = pl.ds(pl.multiple_of(i * tile, tile), tile)
        return [
            pltpu.make_async_copy(sums.at[k, at], dst.at[0, at], out_sem.at[k, i])
            for k, dst in enumerate((g_gate, g_up, g_down))
        ]

    for i in range(count):
        for c in load(i):
            c.start()
    small_in = pltpu.make_async_copy(summed, small, small_sem.at[0])
    small_in.start()
    item_in.wait()
    for u in range(p.spans):
        for i, kind in enumerate((2, 0, 1)):
            for t in range(p.col_tiles):
                at = u * p.span + t * LANES
                piece = items[KINDS * u + i, t * p.row_split : (t + 1) * p.row_split]
                acts[kind, :, at : at + LANES] = piece.reshape(p.padded, LANES)[: p.slots]
    small_in.wait()
    small_out = pltpu.make_async_copy(small, out, small_sem.at[1])
    small_out.start()

    @pl.loop(0, count)
    def _(i):
        at = pl.ds(pl.multiple_of(i * tile, tile), tile)
        for c in load(i):
            c.wait()
        for k, src in enumerate((x, x, g)):
            sums[k, at, :] = jnp.dot(src[at, :], acts[k], preferred_element_type=jnp.float32)
        for c in store(i):
            c.start()

    small_out.wait()

    @pl.loop(0, count)
    def _(i):
        for c in store(i):
            c.wait()


def finish(p, landed, rows, grads, summed):
    tile = min(256, p.model)
    grad_shape = jax.ShapeDtypeStruct((1, p.model, p.hidden), jnp.float32)
    anywhere = pl.BlockSpec(memory_space=pl.ANY)
    dma = pltpu.SemaphoreType.DMA
    return pl.pallas_call(
        functools.partial(final_kernel, p),
        out_shape=(
            grad_shape,
            grad_shape,
            grad_shape,
            jax.ShapeDtypeStruct(summed.shape, summed.dtype),
        ),
        in_specs=[anywhere] * 4,
        out_specs=[anywhere] * 4,
        scratch_shapes=[
            pltpu.VMEM(landed.shape, landed.dtype),
            pltpu.VMEM(rows.shape, rows.dtype),
            pltpu.VMEM(grads.shape, grads.dtype),
            pltpu.VMEM(summed.shape, summed.dtype),
            pltpu.VMEM((KINDS, p.slots, p.hidden), landed.dtype),
            pltpu.VMEM((KINDS, p.model, p.hidden), jnp.float32),
            dma,
            dma((p.model // tile,)),
            dma((p.model // tile,)),
            dma((2,)),
            dma((KINDS, p.model // tile)),
        ],
    )(landed, rows, grads, summed)


def local(n_expert, n_dp, tokens, cotangent, routes, probs, matching, w_gate, w_up, w_down):
    tok_rows, top_count = routes.shape
    p = Plan(n_expert, n_dp, tok_rows, tokens.shape[1], top_count, w_gate.shape[2])
    operands = (matching, tokens, cotangent, routes.T, probs.T, w_gate, w_up, w_down)
    sizes = (p.half // 2, 3 * p.half // 4, p.half)
    pairs = jnp.sum((matching[: p.half] >= p.half).astype(jnp.int32))
    which = sum((pairs > size).astype(jnp.int32) for size in sizes[:-1])
    calls = [
        functools.partial(lambda size, i, *a: communicate(p, size, i, a), size, i)
        for i, size in enumerate(sizes)
    ]
    landed, rows, grads, summed = lax.switch(which, calls, *operands)
    g_gate, g_up, g_down, input_grad = finish(p, landed, rows, grads, summed)
    return input_grad, g_gate, g_up, g_down


def solution(mesh):
    weights = P("expert", None, "dp")
    return jax.shard_map(
        functools.partial(local, mesh.shape["expert"], mesh.shape["dp"]),
        mesh=mesh,
        in_specs=(
            P("expert", "dp"),
            P("expert", "dp"),
            P("expert", None),
            P("expert", None),
            P(),
            weights,
            weights,
            weights,
        ),
        out_specs=(P("expert", "dp"), weights, weights, weights),
        check_vma=False,
    )
```

```python
import functools
import math

import jax
import jax.numpy as jnp
from jax import lax
from jax.experimental import pallas as pl
from jax.experimental.pallas import tpu as pltpu
from jax.sharding import PartitionSpec as P

contract_cols = (((1,), (1,)), ((), ()))
MESH = pl.DeviceIdType.MESH
KINDS = 3
LANES = 128


def bit_count(size):
    return size.bit_length() - 1


def gather_orders(expert_bits, dp_bits):
    far = [("expert", b) for b in range(expert_bits - 1, 1, -1)]
    mid = [("expert", 1)]
    last = [("expert", 0)]
    across = [("dp", b) for b in range(dp_bits)]
    return (
        far + across + mid + last,
        across + far + mid + last,
        far + mid + across + last,
        mid + far + across + last,
        far + mid + last,
    )


def landing_order(steps, parts):
    def turn(mask):
        top = 2 ** (mask.bit_length() - 1)
        return (mask - top, top)

    return [(i, mask) for mask in sorted(range(1, 2 ** (steps - 1)), key=turn) for i in range(parts)]


def reduce_orders(expert_bits, dp_bits):
    far = [("expert", b) for b in range(2, expert_bits)]
    mid = [("expert", 1)]
    near = [("expert", 0)]
    across = [("dp", b) for b in range(dp_bits - 1, -1, -1)]
    return (near + across + mid + far, near + mid + across + far)


def reduce_shapes(order, expert_bits, dp_bits, rows, width):
    left_e, left_d = expert_bits, dp_bits
    shapes = []
    for axis, _ in order:
        if axis == "expert":
            left_e -= 1
        else:
            left_d -= 1
        shapes.append((2,) * left_e + (rows, width * 2**left_d))
    return shapes


class Plan:
    def __init__(self, n_expert, n_dp, tok_rows, width, top_count, hidden):
        self.n_expert, self.n_dp = n_expert, n_dp
        self.expert_bits, self.dp_bits = bit_count(n_expert), bit_count(n_dp)
        self.tok_rows, self.width, self.hidden = tok_rows, width, hidden
        self.top_count = top_count
        self.model = width * n_dp
        self.total = n_expert * tok_rows
        self.capacity = max(2, 5 * tok_rows * top_count // (4 * n_expert))
        self.blocks = 16 // math.gcd(16, self.capacity)
        self.groups = n_expert // self.blocks
        self.group_slots = self.blocks * self.capacity
        self.group_toks = self.blocks * tok_rows
        self.slots = self.groups * self.group_slots
        self.half = n_expert // 2
        self.span = min(256, hidden)
        self.spans = hidden // self.span
        self.chunks = KINDS * self.spans
        self.col_tiles = self.span // LANES
        self.row_split = self.half // self.col_tiles
        unit = 16 * self.row_split
        self.padded = -(-self.slots // unit) * unit
        self.piece_rows = self.padded // self.row_split
        self.row_tile = min(256, self.total)
        self.steps = self.expert_bits + self.dp_bits
        self.row_parts = 2 if 2**self.steps <= 128 else 1


def comm_kernel(
    p,
    crossing,
    match,
    tokens,
    cotangent,
    routes,
    probs,
    h_gate,
    h_up,
    h_down,
    landed,
    out_rows,
    out_grads,
    result,
    *scratch,
):
    n, half = p.n_expert, p.half
    steps, chunks = p.steps, p.chunks
    halves = 2
    sums = [scratch[i * steps : (i + 1) * steps] for i in range(halves)]
    came = [scratch[(halves + i) * steps : (halves + i + 1) * steps] for i in range(halves)]
    rest = scratch[2 * halves * steps :]
    arrived = rest[:chunks]
    swapped = rest[chunks : 2 * chunks]
    staged = rest[2 * chunks : 3 * chunks]
    ordered = rest[3 * chunks : 4 * chunks]
    (
        all_tok,
        all_cot,
        all_routes,
        all_probs,
        w_gate,
        w_up,
        w_down,
        weights,
        p_weights,
        picks,
        p_picks,
        gates,
        uppers,
        backs,
        packed,
        index,
        part,
        x_rows,
        x_cols,
        g_cols,
        summed,
        gsend,
        grecv,
        msend,
        mrecv,
        own,
        wsem,
        send1,
        recv1,
        send2,
        recv2,
        send3,
        recv3,
        stay1,
        stay3,
        rsend,
        rrecv,
        osem,
    ) = rest[4 * chunks :]
    e = lax.axis_index("expert")
    d = lax.axis_index("dp")
    h = e % half
    base = e - h
    step_of = [2**b * (1 - 2 * ((e // 2**b) % 2)) for b in range(p.expert_bits)]
    step_dp = [2**b * (1 - 2 * ((d // 2**b) % 2)) for b in range(p.dp_bits)]
    rows_half = p.tok_rows // 2
    part_rows = p.tok_rows // p.row_parts
    width = p.width

    def peer(axis, bit):
        if axis == "expert":
            return (d, e + step_of[bit])
        return (d + step_dp[bit], e)

    def origin(order, mask):
        at_e, at_d = e, d
        for k, (axis, bit) in enumerate(order):
            if mask >> k & 1:
                if axis == "expert":
                    at_e = at_e + step_of[bit]
                else:
                    at_d = at_d + step_dp[bit]
        return at_e, at_d

    orders = gather_orders(p.expert_bits, p.dp_bits)
    sources = (
        (tokens, all_tok, 0, orders[0]),
        (cotangent, all_cot, 0, orders[1]),
        (tokens, all_tok, 1, orders[2]),
        (cotangent, all_cot, 1, orders[3]),
    )[: 2 * p.row_parts]

    def block(dst, index, at_e, at_d):
        row = pl.multiple_of(at_e * p.tok_rows + index * part_rows, part_rows)
        col = pl.multiple_of(at_d * width, width)
        return dst.at[pl.ds(row, part_rows), pl.ds(col, width)]

    metas = ((routes, all_routes), (probs, all_probs))
    locals_ = []
    for i, (src, dst) in enumerate(((tokens, all_tok), (cotangent, all_cot))):
        row = pl.multiple_of(e * p.tok_rows, p.tok_rows)
        col = pl.multiple_of(d * width, width)
        c = pltpu.make_async_copy(
            src, dst.at[pl.ds(row, p.tok_rows), pl.ds(col, width)], own.at[i]
        )
        c.start()
        locals_.append(c)
    for i, (src, dst) in enumerate(metas):
        c = pltpu.make_async_copy(src, dst.at[e], own.at[2 + i])
        c.start()
        locals_.append(c)

    barrier = pltpu.get_barrier_semaphore()

    @pl.loop(1, half)
    def _(o):
        pl.semaphore_signal(
            barrier, inc=1, device_id=(d, base + (h + o) % half), device_id_type=MESH
        )

    mirror = (d, (e + half) % n)
    pl.semaphore_signal(barrier, inc=1, device_id=mirror, device_id_type=MESH)
    for b in range(p.dp_bits):
        pl.semaphore_signal(barrier, inc=1, device_id=(d + step_dp[b], e), device_id_type=MESH)
    other = (base + half) % n
    full = crossing == half

    def cross_list(start):
        flags, counts, count = [], [], 0
        for i in range(half):
            m = match[start + i]
            flag = jnp.where((m >= start) & (m < start + half), 0, 1)
            flags.append(flag)
            counts.append(count)
            count = count + flag
        return flags, counts

    if not full:
        mine, theirs = cross_list(base), cross_list(other)
    for k in range(half):
        found = k
        if not full:
            found = 0
            for i in range(half):
                found = found + jnp.where((mine[0][i] == 1) & (mine[1][i] == k), i, 0)
        m = match[base + k]
        inside = (m >= base) & (m < base + half)
        far = m - other
        if not full:
            far = 0
            for i in range(half):
                far = far + jnp.where(m - other == i, theirs[1][i], 0)
        index[0, k] = found
        index[1, k] = jnp.where(inside, m - base, 0)
        index[2, k] = jnp.where(inside, 0, far)
        index[3, k] = jnp.where(inside, 1, 0)

    pl.semaphore_wait(barrier, half + p.dp_bits)

    def flight(i, mask, k):
        src, dst, index, order = sources[i]
        at = block(dst, index, *origin(order, mask))
        if mask == 0:
            src = src.at[pl.ds(index * part_rows, part_rows)]
        else:
            src = at
        got = mask + 2**k
        return pltpu.make_async_remote_copy(
            src_ref=src,
            dst_ref=at,
            send_sem=gsend.at[i, got],
            recv_sem=grecv.at[i, got],
            device_id=peer(*order[k]),
            device_id_type=MESH,
        )

    def meta_flight(i, mask, k):
        src, dst = metas[i]
        at = dst.at[origin(orders[4], mask)[0]]
        got = mask + 2**k
        return pltpu.make_async_remote_copy(
            src_ref=src if mask == 0 else at,
            dst_ref=at,
            send_sem=msend.at[i, got],
            recv_sem=mrecv.at[i, got],
            device_id=peer(*orders[4][k]),
            device_id_type=MESH,
        )

    flights, meta_flights = {}, {}

    def send_on(i, mask):
        top = mask.bit_length()
        for k in range(top, steps):
            c = flight(i, mask, k)
            c.start()
            flights[i, mask + 2**k] = c

    def meta_on(i, mask):
        for k in range(mask.bit_length(), p.expert_bits):
            c = meta_flight(i, mask, k)
            c.start()
            meta_flights[i, mask + 2**k] = c

    for i in range(len(metas)):
        meta_on(i, 0)
    for k in range(steps):
        for i in range(len(sources)):
            c = flight(i, 0, k)
            c.start()
            flights[i, 2**k] = c
    loads = []
    for i, (src, dst) in enumerate(((h_gate, w_gate), (h_up, w_up), (h_down, w_down))):
        c = pltpu.make_async_copy(src, dst, wsem.at[i])
        c.start()
        loads.append(c)

    meta_masks = list(range(1, 2**p.expert_bits))
    for count, (i, mask) in enumerate(landing_order(steps, len(sources))):
        flights[i, mask].wait_recv()
        send_on(i, mask)
        if count % len(sources) == len(sources) - 1 and meta_masks:
            meta = meta_masks.pop(0)
            for k in range(len(metas)):
                meta_flights[k, meta].wait_recv()
                meta_on(k, meta)
    for meta in meta_masks:
        for k in range(len(metas)):
            meta_flights[k, meta].wait_recv()
            meta_on(k, meta)
    for c in locals_:
        c.wait()

    partner = match[e]
    tok = p.tok_rows
    at = lax.broadcasted_iota(jnp.int32, (tok, tok), 0)
    to = lax.broadcasted_iota(jnp.int32, (tok, tok), 1)
    before = jnp.where(at < to, 1.0, 0.0).astype(jnp.bfloat16)
    start = (lax.broadcasted_iota(jnp.int32, (n, tok), 0) % p.blocks) * p.capacity
    tables = []
    for who in (e, partner):
        hit = all_routes[...] == who
        w = jnp.sum(jnp.where(hit, all_probs[...], 0.0), axis=1)
        f = jnp.sum(jnp.where(hit, 1.0, 0.0), axis=1)
        rank = jnp.dot(f.astype(jnp.bfloat16), before, preferred_element_type=jnp.float32)
        place = jnp.where(f > 0.5, rank + start.astype(jnp.float32), -1.0)
        tables.append((jnp.transpose(w), jnp.transpose(place)))
    for (w, place), w_ref, pick_ref in (
        (tables[0], weights, picks),
        (tables[1], p_weights, p_picks),
    ):
        for g in range(p.groups):
            cols = []
            for b in range(g * p.blocks, (g + 1) * p.blocks):
                w_ref[b * tok : (b + 1) * tok, :] = jnp.broadcast_to(w[:, b : b + 1], (tok, LANES))
                cols.append(jnp.broadcast_to(place[:, b : b + 1], (tok, LANES)))
            spots = jnp.concatenate(cols, axis=0)
            lane = lax.broadcasted_iota(jnp.int32, spots.shape, 1).astype(jnp.float32)
            hot = jnp.transpose(jnp.where(spots == lane, 1.0, 0.0))
            pick_ref[g] = hot[: p.group_slots].astype(jnp.bfloat16)

    for mask in range(2 ** (steps - 1), 2**steps):
        for i in range(len(sources)):
            flights[i, mask].wait_recv()
    for c in loads:
        c.wait()

    tiles = p.total // p.row_tile
    tile_bits = bit_count(tiles)

    def tile_of(t):
        return tuple((t >> (tile_bits - 1 - i)) & 1 for i in range(tile_bits))

    def scale():
        for t in range(tiles):
            rows = slice(t * p.row_tile, (t + 1) * p.row_tile)
            value = (all_cot[rows, :].astype(jnp.float32) * weights[rows, :][:, :1]).astype(
                jnp.bfloat16
            )
            shape = part.shape[tile_bits:]
            part[tile_of(t)] = value.reshape(shape)

    def first_half(u):
        cols = slice(u * p.span, (u + 1) * p.span)
        for t in range(tiles):
            rows = slice(t * p.row_tile, (t + 1) * p.row_tile)
            x = all_tok[rows, :]
            gate = jnp.dot(x, w_gate[0, :, cols], preferred_element_type=jnp.float32)
            upper = jnp.dot(x, w_up[0, :, cols], preferred_element_type=jnp.float32)
            gates[rows, :] = gate
            uppers[rows, :] = upper
            backs[2, rows, cols] = (gate * jax.nn.sigmoid(gate) * upper).astype(jnp.bfloat16)

    def second_half(u):
        cols = slice(u * p.span, (u + 1) * p.span)
        for t in range(tiles):
            rows = slice(t * p.row_tile, (t + 1) * p.row_tile)
            grads = part[tile_of(t)].reshape(p.row_tile, p.model)
            back = jnp.dot(grads, w_down[0, :, cols], preferred_element_type=jnp.float32)
            gate = gates[rows, :]
            sig = jax.nn.sigmoid(gate)
            backs[0, rows, cols] = (
                back * uppers[rows, :] * sig * (1.0 + gate * (1.0 - sig))
            ).astype(jnp.bfloat16)
            backs[1, rows, cols] = (back * gate * sig).astype(jnp.bfloat16)

    def pack(c, kind, u):
        per = p.group_slots // p.piece_rows
        for g in range(p.groups):
            rows = slice(g * p.group_toks, (g + 1) * p.group_toks)
            value = backs[kind, rows, u * p.span : (u + 1) * p.span]
            value = jnp.dot(picks[g], value, preferred_element_type=jnp.float32)
            value = value.astype(jnp.bfloat16)
            for t in range(p.col_tiles):
                j = t * p.row_split + g * per
                packed[c, j : j + per] = value[:, t * LANES : (t + 1) * LANES].reshape(
                    per, p.piece_rows, LANES
                )
        spare = p.row_split - p.groups * per
        if spare:
            for t in range(p.col_tiles):
                j = (t + 1) * p.row_split
                packed[c, j - spare : j] = jnp.zeros((spare, p.piece_rows, LANES), jnp.bfloat16)

    def spread(c, o):
        to_h = (h + o) % half
        return pltpu.make_async_remote_copy(
            src_ref=packed.at[c, to_h],
            dst_ref=arrived[c].at[h],
            send_sem=send1.at[c, o],
            recv_sem=recv1.at[c, o],
            device_id=(d, base + to_h),
            device_id_type=MESH,
        )

    def swap(c):
        return pltpu.make_async_remote_copy(
            src_ref=staged[c],
            dst_ref=swapped[c],
            send_sem=send2.at[c],
            recv_sem=recv2.at[c],
            device_id=mirror,
            device_id_type=MESH,
        )

    def collect(c, o):
        to_h = (h + o) % half
        return pltpu.make_async_remote_copy(
            src_ref=ordered[c].at[to_h],
            dst_ref=landed.at[c, h],
            send_sem=send3.at[c, o],
            recv_sem=recv3.at[c, o],
            device_id=(d, base + to_h),
            device_id_type=MESH,
        )

    def stay_first(c):
        return pltpu.make_async_copy(packed.at[c, h], arrived[c].at[h], stay1.at[c])

    def stay_last(c):
        return pltpu.make_async_copy(ordered[c].at[h], landed.at[c, h], stay3.at[c])

    def begin(c, kind, u):
        pack(c, kind, u)
        stay_first(c).start()

        @pl.loop(1, half)
        def _(o):
            spread(c, o).start()

    def swap_on(c):
        stay_first(c).wait()

        @pl.loop(1, half)
        def _(o):
            spread(c, o).wait_recv()

        if full:
            staged[c][...] = arrived[c][...]
        else:
            for k in range(crossing):
                staged[c][k] = arrived[c][index[0, k]]
        swap(c).start()

    def collect_on(c):
        swap(c).wait_recv()
        for i in range(half):
            near = arrived[c][index[1, i]]
            far = swapped[c][index[2, i]]
            ordered[c][i] = jnp.where(index[3, i] == 1, near, far)
        stay_last(c).start()

        @pl.loop(1, half)
        def _(o):
            collect(c, o).start()

    r_orders = reduce_orders(p.expert_bits, p.dp_bits)
    r_flights = [[], []]

    def split(i, s):
        axis, bit = r_orders[i][s]
        if s == 0:
            ref, rows = part, pl.ds(i * rows_half, rows_half)
        else:
            ref, rows = sums[i][s - 1], slice(None)
        left = [b for a, b in r_orders[i][s:] if a == "expert"]
        left = sorted(left, reverse=True)
        if axis == "expert":
            mine = (e // 2**bit) % 2
            spot = left.index(bit)

            def where(v):
                return tuple(
                    [slice(None)] * spot + [v] + [slice(None)] * (len(left) - spot - 1)
                ) + (rows, slice(None))

            return ref, where(mine), where(1 - mine)
        mine = (d // 2**bit) % 2
        span = 2**bit * width
        head = (slice(None),) * len(left) + (rows,)
        keep = head + (pl.ds(pl.multiple_of(mine * span, LANES), span),)
        give = head + (pl.ds(pl.multiple_of((1 - mine) * span, LANES), span),)
        return ref, keep, give

    def start_step(i, s):
        ref, _, give = split(i, s)
        c = pltpu.make_async_remote_copy(
            src_ref=ref.at[give],
            dst_ref=came[i][s],
            send_sem=rsend.at[i, s],
            recv_sem=rrecv.at[i, s],
            device_id=peer(*r_orders[i][s]),
            device_id_type=MESH,
        )
        c.start()
        r_flights[i].append(c)

    def end_step(i, s):
        ref, keep, _ = split(i, s)
        r_flights[i][s].wait_recv()
        total = ref[keep].astype(jnp.float32) + came[i][s][...].astype(jnp.float32)
        sums[i][s][...] = total.astype(sums[i][s].dtype)

    def next_step(s):
        for i in range(halves):
            end_step(i, s)
            if s + 1 < steps:
                start_step(i, s + 1)

    def pack_rows(src, dst, w_ref):
        span = min(512, p.model)

        @pl.loop(0, p.model // span)
        def _(t):
            cols = pl.ds(pl.multiple_of(t * span, span), span)
            for g in range(p.groups):
                rows = slice(g * p.group_toks, (g + 1) * p.group_toks)
                at_rows = slice(g * p.group_slots, (g + 1) * p.group_slots)
                x = src[rows, cols]
                if w_ref is not None:
                    x = (x.astype(jnp.float32) * w_ref[rows, :][:, :1]).astype(jnp.bfloat16)
                x_rows[at_rows, :] = jnp.dot(
                    p_picks[g], x, preferred_element_type=jnp.float32
                ).astype(jnp.bfloat16)
            dst[cols, :] = jnp.transpose(x_rows[...])

    def make_part(first, last):
        tile = min(512, p.model)

        @pl.loop(first * p.model // (2 * tile), last * p.model // (2 * tile))
        def _(t):
            cols = pl.ds(pl.multiple_of(t * tile, tile), tile)
            piece = lax.dot_general(
                backs[0], w_gate[0, cols, :], contract_cols, preferred_element_type=jnp.float32
            )
            piece += lax.dot_general(
                backs[1], w_up[0, cols, :], contract_cols, preferred_element_type=jnp.float32
            )
            shape = part.shape[:-1] + (tile,)
            part[..., cols] = piece.astype(part.dtype).reshape(shape)

    for u in range(p.spans):
        first_half(u)
        begin(KINDS * u, 2, u)
        if u == 0:
            scale()
        second_half(u)
        begin(KINDS * u + 1, 0, u)
        begin(KINDS * u + 2, 1, u)
    make_part(0, 1)
    swap_on(0)
    make_part(1, 2)
    for i in range(halves):
        start_step(i, 0)
    for c in range(1, KINDS):
        swap_on(c)
    next_step(0)
    for c in range(KINDS, chunks):
        swap_on(c)
    pack_rows(all_tok, x_cols, None)
    row_out = pltpu.make_async_copy(x_cols, out_rows, osem.at[0])
    row_out.start()
    pace = 42 * crossing / (half * chunks)
    events = [(10 + pace * (c + 1), 0, c) for c in range(chunks)]
    events += [(12 + 6.5 * s, 1, s) for s in range(1, steps)]
    events.append((10 + 1.1 * pace, 2, 0))
    for _, kind, which in sorted(events):
        if kind == 0:
            collect_on(which)
        elif kind == 1:
            next_step(which)
        else:
            pack_rows(all_cot, g_cols, p_weights)
            grad_out = pltpu.make_async_copy(g_cols, out_grads, osem.at[1])
            grad_out.start()
    for i in range(halves):
        summed[pl.ds(i * rows_half, rows_half), :] = sums[i][steps - 1][...]
    result_out = pltpu.make_async_copy(summed, result, osem.at[2])
    result_out.start()

    for c in flights.values():
        c.wait_send()
    for c in meta_flights.values():
        c.wait_send()
    for f in r_flights:
        for c in f:
            c.wait_send()
    row_out.wait()
    grad_out.wait()
    result_out.wait()
    for c in range(chunks):
        stay_last(c).wait()
        swap(c).wait_send()

        @pl.loop(1, half)
        def _(o):
            spread(c, o).wait_send()
            collect(c, o).wait_send()
            collect(c, o).wait_recv()


def communicate(p, crossing, call_id, operands):
    dtype = operands[1].dtype
    reduce_buffers = []
    for order in reduce_orders(p.expert_bits, p.dp_bits):
        for shape in reduce_shapes(order, p.expert_bits, p.dp_bits, p.tok_rows // 2, p.width):
            reduce_buffers.append(pltpu.VMEM(shape, dtype))
    piece = (p.piece_rows, LANES)
    weight = operands[-1].shape
    dma = pltpu.SemaphoreType.DMA
    steps, chunks, half = p.steps, p.chunks, p.half
    scratch = (
        reduce_buffers
        + reduce_buffers
        + [pltpu.VMEM((half,) + piece, dtype)] * chunks
        + [pltpu.VMEM((crossing,) + piece, dtype)] * (2 * chunks)
        + [pltpu.VMEM((half,) + piece, dtype)] * chunks
        + [
            pltpu.VMEM((p.total, p.model), dtype),
            pltpu.VMEM((p.total, p.model), dtype),
            pltpu.VMEM((p.n_expert, p.top_count, p.tok_rows), jnp.int32),
            pltpu.VMEM((p.n_expert, p.top_count, p.tok_rows), jnp.float32),
            pltpu.VMEM(weight, dtype),
            pltpu.VMEM(weight, dtype),
            pltpu.VMEM(weight, dtype),
            pltpu.VMEM((p.total, LANES), jnp.float32),
            pltpu.VMEM((p.total, LANES), jnp.float32),
            pltpu.VMEM((p.groups, p.group_slots, p.group_toks), dtype),
            pltpu.VMEM((p.groups, p.group_slots, p.group_toks), dtype),
            pltpu.VMEM((p.total, p.span), jnp.float32),
            pltpu.VMEM((p.total, p.span), jnp.float32),
            pltpu.VMEM((KINDS, p.total, p.hidden), dtype),
            pltpu.VMEM((chunks, half) + piece, dtype),
            pltpu.SMEM((4, half), jnp.int32),
            pltpu.VMEM((2,) * p.expert_bits + (p.tok_rows, p.model), dtype),
            pltpu.VMEM((p.slots, min(512, p.model)), dtype),
            pltpu.VMEM((p.model, p.slots), dtype),
            pltpu.VMEM((p.model, p.slots), dtype),
            pltpu.VMEM((p.tok_rows, p.width), dtype),
            dma((2 * p.row_parts, 2**steps)),
            dma((2 * p.row_parts, 2**steps)),
            dma((2, p.n_expert)),
            dma((2, p.n_expert)),
            dma((4,)),
            dma((3,)),
            dma((chunks, half)),
            dma((chunks, half)),
            dma((chunks,)),
            dma((chunks,)),
            dma((chunks, half)),
            dma((chunks, half)),
            dma((chunks,)),
            dma((chunks,)),
            dma((2, steps)),
            dma((2, steps)),
            dma((3,)),
        ]
    )
    anywhere = pl.BlockSpec(memory_space=pl.ANY)
    return pl.pallas_call(
        functools.partial(comm_kernel, p, crossing),
        out_shape=(
            jax.ShapeDtypeStruct((chunks, half) + piece, dtype),
            jax.ShapeDtypeStruct((p.model, p.slots), dtype),
            jax.ShapeDtypeStruct((p.model, p.slots), dtype),
            jax.ShapeDtypeStruct((p.tok_rows, p.width), dtype),
        ),
        in_specs=[pl.BlockSpec(memory_space=pltpu.SMEM)] + [anywhere] * 7,
        out_specs=[anywhere] * 4,
        scratch_shapes=scratch,
        compiler_params=pltpu.CompilerParams(
            collective_id=call_id, has_side_effects=True, vmem_limit_bytes=64 * 2**20 - 2**16
        ),
    )(*operands)


def final_kernel(
    p, landed, rows, grads, summed, g_gate, g_up, g_down, out, items, x, g, small, acts, sums,
    item_sem, x_sem, g_sem, small_sem, out_sem,
):
    tile = min(512, p.model)
    count = p.model // tile
    item_in = pltpu.make_async_copy(landed, items, item_sem)
    item_in.start()

    def load(i):
        at = pl.ds(pl.multiple_of(i * tile, tile), tile)
        return (
            pltpu.make_async_copy(rows.at[at], x.at[at], x_sem.at[i]),
            pltpu.make_async_copy(grads.at[at], g.at[at], g_sem.at[i]),
        )

    def store(i):
        at = pl.ds(pl.multiple_of(i * tile, tile), tile)
        return [
            pltpu.make_async_copy(sums.at[k, at], dst.at[0, at], out_sem.at[k, i])
            for k, dst in enumerate((g_gate, g_up, g_down))
        ]

    for i in range(count):
        for c in load(i):
            c.start()
    small_in = pltpu.make_async_copy(summed, small, small_sem.at[0])
    small_in.start()
    item_in.wait()
    for u in range(p.spans):
        for i, kind in enumerate((2, 0, 1)):
            for t in range(p.col_tiles):
                at = u * p.span + t * LANES
                piece = items[KINDS * u + i, t * p.row_split : (t + 1) * p.row_split]
                acts[kind, :, at : at + LANES] = piece.reshape(p.padded, LANES)[: p.slots]
    small_in.wait()
    small_out = pltpu.make_async_copy(small, out, small_sem.at[1])
    small_out.start()

    @pl.loop(0, count)
    def _(i):
        at = pl.ds(pl.multiple_of(i * tile, tile), tile)
        for c in load(i):
            c.wait()
        outs = store(i)
        for k, src in enumerate((x, x, g)):
            sums[k, at, :] = jnp.dot(src[at, :], acts[k], preferred_element_type=jnp.float32)
            outs[k].start()

    small_out.wait()

    @pl.loop(0, count)
    def _(i):
        for c in store(i):
            c.wait()


def finish(p, landed, rows, grads, summed):
    tile = min(512, p.model)
    grad_shape = jax.ShapeDtypeStruct((1, p.model, p.hidden), jnp.float32)
    anywhere = pl.BlockSpec(memory_space=pl.ANY)
    dma = pltpu.SemaphoreType.DMA
    return pl.pallas_call(
        functools.partial(final_kernel, p),
        out_shape=(
            grad_shape,
            grad_shape,
            grad_shape,
            jax.ShapeDtypeStruct(summed.shape, summed.dtype),
        ),
        in_specs=[anywhere] * 4,
        out_specs=[anywhere] * 4,
        scratch_shapes=[
            pltpu.VMEM(landed.shape, landed.dtype),
            pltpu.VMEM(rows.shape, rows.dtype),
            pltpu.VMEM(grads.shape, grads.dtype),
            pltpu.VMEM(summed.shape, summed.dtype),
            pltpu.VMEM((KINDS, p.slots, p.hidden), landed.dtype),
            pltpu.VMEM((KINDS, p.model, p.hidden), jnp.float32),
            dma,
            dma((p.model // tile,)),
            dma((p.model // tile,)),
            dma((2,)),
            dma((KINDS, p.model // tile)),
        ],
    )(landed, rows, grads, summed)


def local(n_expert, n_dp, tokens, cotangent, routes, probs, matching, w_gate, w_up, w_down):
    tok_rows, top_count = routes.shape
    p = Plan(n_expert, n_dp, tok_rows, tokens.shape[1], top_count, w_gate.shape[2])
    operands = (matching, tokens, cotangent, routes.T, probs.T, w_gate, w_up, w_down)
    sizes = (p.half // 2, 3 * p.half // 4, p.half)
    low = jnp.arange(n_expert) < p.half
    crossed = jnp.sum((low != (matching < p.half)).astype(jnp.int32))
    over = jnp.maximum(crossed - (p.half // 2 + 1), 0)
    which = lax.shift_right_logical(over, bit_count(p.half // 2))
    calls = [
        functools.partial(lambda size, i, *a: communicate(p, size, i, a), size, i)
        for i, size in enumerate(sizes)
    ]
    landed, rows, grads, summed = lax.switch(which, calls, *operands)
    g_gate, g_up, g_down, input_grad = finish(p, landed, rows, grads, summed)
    return input_grad, g_gate, g_up, g_down


def solution(mesh):
    weights = P("expert", None, "dp")
    return jax.shard_map(
        functools.partial(local, mesh.shape["expert"], mesh.shape["dp"]),
        mesh=mesh,
        in_specs=(
            P("expert", "dp"),
            P("expert", "dp"),
            P("expert", None),
            P("expert", None),
            P(),
            weights,
            weights,
            weights,
        ),
        out_specs=(P("expert", "dp"), weights, weights, weights),
        check_vma=False,
    )
```

```python
import functools
import math

import jax
import jax.numpy as jnp
from jax import lax
from jax.experimental import pallas as pl
from jax.experimental.pallas import tpu as pltpu
from jax.sharding import PartitionSpec as P

contract_cols = (((1,), (1,)), ((), ()))
MESH = pl.DeviceIdType.MESH
KINDS = 3
LANES = 128


def bit_count(size):
    return size.bit_length() - 1


def gather_orders(expert_bits, dp_bits):
    far = [("expert", b) for b in range(expert_bits - 1, 1, -1)]
    mid = [("expert", 1)]
    last = [("expert", 0)]
    across = [("dp", b) for b in range(dp_bits)]
    return (
        far + across + mid + last,
        across + far + mid + last,
        far + mid + across + last,
        mid + far + across + last,
        far + mid + last,
    )


def landing_order(steps, parts):
    def turn(mask):
        top = 2 ** (mask.bit_length() - 1)
        return (mask - top, top)

    return [(i, mask) for mask in sorted(range(1, 2 ** (steps - 1)), key=turn) for i in range(parts)]


def reduce_orders(expert_bits, dp_bits):
    far = [("expert", b) for b in range(2, expert_bits)]
    mid = [("expert", 1)]
    near = [("expert", 0)]
    across = [("dp", b) for b in range(dp_bits - 1, -1, -1)]
    return (near + across + mid + far, near + mid + across + far)


def reduce_shapes(order, expert_bits, dp_bits, rows, width):
    left_e, left_d = expert_bits, dp_bits
    shapes = []
    for axis, _ in order:
        if axis == "expert":
            left_e -= 1
        else:
            left_d -= 1
        shapes.append((2,) * left_e + (rows, width * 2**left_d))
    return shapes


class Plan:
    def __init__(self, n_expert, n_dp, tok_rows, width, top_count, hidden):
        self.n_expert, self.n_dp = n_expert, n_dp
        self.expert_bits, self.dp_bits = bit_count(n_expert), bit_count(n_dp)
        self.tok_rows, self.width, self.hidden = tok_rows, width, hidden
        self.top_count = top_count
        self.model = width * n_dp
        self.total = n_expert * tok_rows
        self.capacity = max(2, 5 * tok_rows * top_count // (4 * n_expert))
        self.blocks = 16 // math.gcd(16, self.capacity)
        self.groups = n_expert // self.blocks
        self.group_slots = self.blocks * self.capacity
        self.group_toks = self.blocks * tok_rows
        self.slots = self.groups * self.group_slots
        self.half = n_expert // 2
        self.span = min(256, hidden)
        self.spans = hidden // self.span
        self.chunks = KINDS * self.spans
        self.col_tiles = self.span // LANES
        self.row_split = self.half // self.col_tiles
        unit = 16 * self.row_split
        self.padded = -(-self.slots // unit) * unit
        self.piece_rows = self.padded // self.row_split
        self.row_tile = min(256, self.total)
        self.steps = self.expert_bits + self.dp_bits
        self.row_parts = 2 if 2**self.steps <= 128 else 1


def comm_kernel(
    p,
    crossing,
    match,
    tokens,
    cotangent,
    routes,
    probs,
    h_gate,
    h_up,
    h_down,
    landed,
    out_rows,
    out_grads,
    result,
    *scratch,
):
    n, half = p.n_expert, p.half
    steps, chunks = p.steps, p.chunks
    halves = 2
    sums = [scratch[i * steps : (i + 1) * steps] for i in range(halves)]
    came = [scratch[(halves + i) * steps : (halves + i + 1) * steps] for i in range(halves)]
    rest = scratch[2 * halves * steps :]
    arrived = rest[:chunks]
    swapped = rest[chunks : 2 * chunks]
    staged = rest[2 * chunks : 3 * chunks]
    ordered = rest[3 * chunks : 4 * chunks]
    (
        all_tok,
        all_cot,
        all_routes,
        all_probs,
        w_gate,
        w_up,
        w_down,
        weights,
        p_weights,
        picks,
        p_picks,
        gates,
        uppers,
        backs,
        packed,
        index,
        part,
        x_rows,
        x_cols,
        g_cols,
        summed,
        gsend,
        grecv,
        msend,
        mrecv,
        own,
        wsem,
        send1,
        recv1,
        send2,
        recv2,
        send3,
        recv3,
        stay1,
        stay3,
        rsend,
        rrecv,
        osem,
    ) = rest[4 * chunks :]
    e = lax.axis_index("expert")
    d = lax.axis_index("dp")
    h = e % half
    base = e - h
    step_of = [2**b * (1 - 2 * ((e // 2**b) % 2)) for b in range(p.expert_bits)]
    step_dp = [2**b * (1 - 2 * ((d // 2**b) % 2)) for b in range(p.dp_bits)]
    rows_half = p.tok_rows // 2
    part_rows = p.tok_rows // p.row_parts
    width = p.width

    def peer(axis, bit):
        if axis == "expert":
            return (d, e + step_of[bit])
        return (d + step_dp[bit], e)

    def origin(order, mask):
        at_e, at_d = e, d
        for k, (axis, bit) in enumerate(order):
            if mask >> k & 1:
                if axis == "expert":
                    at_e = at_e + step_of[bit]
                else:
                    at_d = at_d + step_dp[bit]
        return at_e, at_d

    orders = gather_orders(p.expert_bits, p.dp_bits)
    sources = (
        (tokens, all_tok, 0, orders[0]),
        (cotangent, all_cot, 0, orders[1]),
        (tokens, all_tok, 1, orders[2]),
        (cotangent, all_cot, 1, orders[3]),
    )[: 2 * p.row_parts]

    def block(dst, index, at_e, at_d):
        row = pl.multiple_of(at_e * p.tok_rows + index * part_rows, part_rows)
        col = pl.multiple_of(at_d * width, width)
        return dst.at[pl.ds(row, part_rows), pl.ds(col, width)]

    metas = ((routes, all_routes), (probs, all_probs))
    locals_ = []
    for i, (src, dst) in enumerate(((tokens, all_tok), (cotangent, all_cot))):
        row = pl.multiple_of(e * p.tok_rows, p.tok_rows)
        col = pl.multiple_of(d * width, width)
        c = pltpu.make_async_copy(
            src, dst.at[pl.ds(row, p.tok_rows), pl.ds(col, width)], own.at[i]
        )
        c.start()
        locals_.append(c)
    for i, (src, dst) in enumerate(metas):
        c = pltpu.make_async_copy(src, dst.at[e], own.at[2 + i])
        c.start()
        locals_.append(c)

    barrier = pltpu.get_barrier_semaphore()

    @pl.loop(1, half)
    def _(o):
        pl.semaphore_signal(
            barrier, inc=1, device_id=(d, base + (h + o) % half), device_id_type=MESH
        )

    mirror = (d, (e + half) % n)
    pl.semaphore_signal(barrier, inc=1, device_id=mirror, device_id_type=MESH)
    for b in range(p.dp_bits):
        pl.semaphore_signal(barrier, inc=1, device_id=(d + step_dp[b], e), device_id_type=MESH)
    other = (base + half) % n
    full = crossing == half

    def cross_list(start):
        flags, counts, count = [], [], 0
        for i in range(half):
            m = match[start + i]
            flag = jnp.where((m >= start) & (m < start + half), 0, 1)
            flags.append(flag)
            counts.append(count)
            count = count + flag
        return flags, counts

    if not full:
        mine, theirs = cross_list(base), cross_list(other)
    for k in range(half):
        found = k
        if not full:
            found = 0
            for i in range(half):
                found = found + jnp.where((mine[0][i] == 1) & (mine[1][i] == k), i, 0)
        m = match[base + k]
        inside = (m >= base) & (m < base + half)
        far = m - other
        if not full:
            far = 0
            for i in range(half):
                far = far + jnp.where(m - other == i, theirs[1][i], 0)
        index[0, k] = found
        index[1, k] = jnp.where(inside, m - base, 0)
        index[2, k] = jnp.where(inside, 0, far)
        index[3, k] = jnp.where(inside, 1, 0)

    pl.semaphore_wait(barrier, half + p.dp_bits)

    def flight(i, mask, k):
        src, dst, index, order = sources[i]
        at = block(dst, index, *origin(order, mask))
        if mask == 0:
            src = src.at[pl.ds(index * part_rows, part_rows)]
        else:
            src = at
        got = mask + 2**k
        return pltpu.make_async_remote_copy(
            src_ref=src,
            dst_ref=at,
            send_sem=gsend.at[i, got],
            recv_sem=grecv.at[i, got],
            device_id=peer(*order[k]),
            device_id_type=MESH,
        )

    def meta_flight(i, mask, k):
        src, dst = metas[i]
        at = dst.at[origin(orders[4], mask)[0]]
        got = mask + 2**k
        return pltpu.make_async_remote_copy(
            src_ref=src if mask == 0 else at,
            dst_ref=at,
            send_sem=msend.at[i, got],
            recv_sem=mrecv.at[i, got],
            device_id=peer(*orders[4][k]),
            device_id_type=MESH,
        )

    flights, meta_flights = {}, {}

    def send_on(i, mask):
        top = mask.bit_length()
        for k in range(top, steps):
            c = flight(i, mask, k)
            c.start()
            flights[i, mask + 2**k] = c

    def meta_on(i, mask):
        for k in range(mask.bit_length(), p.expert_bits):
            c = meta_flight(i, mask, k)
            c.start()
            meta_flights[i, mask + 2**k] = c

    for i in range(len(metas)):
        meta_on(i, 0)
    for k in range(steps):
        for i in range(len(sources)):
            c = flight(i, 0, k)
            c.start()
            flights[i, 2**k] = c
    loads = []
    for i, (src, dst) in enumerate(((h_gate, w_gate), (h_up, w_up), (h_down, w_down))):
        c = pltpu.make_async_copy(src, dst, wsem.at[i])
        c.start()
        loads.append(c)

    meta_masks = list(range(1, 2**p.expert_bits))
    for count, (i, mask) in enumerate(landing_order(steps, len(sources))):
        flights[i, mask].wait_recv()
        send_on(i, mask)
        if count % len(sources) == len(sources) - 1 and meta_masks:
            meta = meta_masks.pop(0)
            for k in range(len(metas)):
                meta_flights[k, meta].wait_recv()
                meta_on(k, meta)
    for meta in meta_masks:
        for k in range(len(metas)):
            meta_flights[k, meta].wait_recv()
            meta_on(k, meta)
    for c in locals_:
        c.wait()

    partner = match[e]
    tok = p.tok_rows
    at = lax.broadcasted_iota(jnp.int32, (tok, tok), 0)
    to = lax.broadcasted_iota(jnp.int32, (tok, tok), 1)
    before = jnp.where(at < to, 1.0, 0.0).astype(jnp.bfloat16)
    start = (lax.broadcasted_iota(jnp.int32, (n, tok), 0) % p.blocks) * p.capacity
    tables = []
    for who in (e, partner):
        hit = all_routes[...] == who
        w = jnp.sum(jnp.where(hit, all_probs[...], 0.0), axis=1)
        f = jnp.sum(jnp.where(hit, 1.0, 0.0), axis=1)
        rank = jnp.dot(f.astype(jnp.bfloat16), before, preferred_element_type=jnp.float32)
        place = jnp.where(f > 0.5, rank + start.astype(jnp.float32), -1.0)
        tables.append((jnp.transpose(w), jnp.transpose(place)))
    for (w, place), w_ref, pick_ref in (
        (tables[0], weights, picks),
        (tables[1], p_weights, p_picks),
    ):
        for g in range(p.groups):
            cols = []
            for b in range(g * p.blocks, (g + 1) * p.blocks):
                w_ref[b * tok : (b + 1) * tok, :] = jnp.broadcast_to(w[:, b : b + 1], (tok, LANES))
                cols.append(jnp.broadcast_to(place[:, b : b + 1], (tok, LANES)))
            spots = jnp.concatenate(cols, axis=0)
            lane = lax.broadcasted_iota(jnp.int32, spots.shape, 1).astype(jnp.float32)
            hot = jnp.transpose(jnp.where(spots == lane, 1.0, 0.0))
            pick_ref[g] = hot[: p.group_slots].astype(jnp.bfloat16)

    for mask in range(2 ** (steps - 1), 2**steps):
        for i in range(len(sources)):
            flights[i, mask].wait_recv()
    for c in loads:
        c.wait()

    tiles = p.total // p.row_tile
    tile_bits = bit_count(tiles)

    def tile_of(t):
        return tuple((t >> (tile_bits - 1 - i)) & 1 for i in range(tile_bits))

    def scale():
        for t in range(tiles):
            rows = slice(t * p.row_tile, (t + 1) * p.row_tile)
            value = (all_cot[rows, :].astype(jnp.float32) * weights[rows, :][:, :1]).astype(
                jnp.bfloat16
            )
            shape = part.shape[tile_bits:]
            part[tile_of(t)] = value.reshape(shape)

    def first_half(u):
        cols = slice(u * p.span, (u + 1) * p.span)
        for t in range(tiles):
            rows = slice(t * p.row_tile, (t + 1) * p.row_tile)
            x = all_tok[rows, :]
            gate = jnp.dot(x, w_gate[0, :, cols], preferred_element_type=jnp.float32)
            upper = jnp.dot(x, w_up[0, :, cols], preferred_element_type=jnp.float32)
            gates[rows, :] = gate
            uppers[rows, :] = upper
            backs[2, rows, cols] = (gate * jax.nn.sigmoid(gate) * upper).astype(jnp.bfloat16)

    def second_half(u):
        cols = slice(u * p.span, (u + 1) * p.span)
        for t in range(tiles):
            rows = slice(t * p.row_tile, (t + 1) * p.row_tile)
            grads = part[tile_of(t)].reshape(p.row_tile, p.model)
            back = jnp.dot(grads, w_down[0, :, cols], preferred_element_type=jnp.float32)
            gate = gates[rows, :]
            sig = jax.nn.sigmoid(gate)
            backs[0, rows, cols] = (
                back * uppers[rows, :] * sig * (1.0 + gate * (1.0 - sig))
            ).astype(jnp.bfloat16)
            backs[1, rows, cols] = (back * gate * sig).astype(jnp.bfloat16)

    def pack(c, kind, u):
        per = p.group_slots // p.piece_rows
        for g in range(p.groups):
            rows = slice(g * p.group_toks, (g + 1) * p.group_toks)
            value = backs[kind, rows, u * p.span : (u + 1) * p.span]
            value = jnp.dot(picks[g], value, preferred_element_type=jnp.float32)
            value = value.astype(jnp.bfloat16)
            for t in range(p.col_tiles):
                j = t * p.row_split + g * per
                packed[c, j : j + per] = value[:, t * LANES : (t + 1) * LANES].reshape(
                    per, p.piece_rows, LANES
                )
        spare = p.row_split - p.groups * per
        if spare:
            for t in range(p.col_tiles):
                j = (t + 1) * p.row_split
                packed[c, j - spare : j] = jnp.zeros((spare, p.piece_rows, LANES), jnp.bfloat16)

    def spread(c, o):
        to_h = (h + o) % half
        return pltpu.make_async_remote_copy(
            src_ref=packed.at[c, to_h],
            dst_ref=arrived[c].at[h],
            send_sem=send1.at[c, o],
            recv_sem=recv1.at[c, o],
            device_id=(d, base + to_h),
            device_id_type=MESH,
        )

    def swap(c):
        return pltpu.make_async_remote_copy(
            src_ref=staged[c],
            dst_ref=swapped[c],
            send_sem=send2.at[c],
            recv_sem=recv2.at[c],
            device_id=mirror,
            device_id_type=MESH,
        )

    def collect(c, o):
        to_h = (h + o) % half
        return pltpu.make_async_remote_copy(
            src_ref=ordered[c].at[to_h],
            dst_ref=landed.at[c, h],
            send_sem=send3.at[c, o],
            recv_sem=recv3.at[c, o],
            device_id=(d, base + to_h),
            device_id_type=MESH,
        )

    def stay_first(c):
        return pltpu.make_async_copy(packed.at[c, h], arrived[c].at[h], stay1.at[c])

    def stay_last(c):
        return pltpu.make_async_copy(ordered[c].at[h], landed.at[c, h], stay3.at[c])

    def begin(c, kind, u):
        pack(c, kind, u)
        stay_first(c).start()

        @pl.loop(1, half)
        def _(o):
            spread(c, o).start()

    def swap_on(c):
        stay_first(c).wait()

        @pl.loop(1, half)
        def _(o):
            spread(c, o).wait_recv()

        if full:
            staged[c][...] = arrived[c][...]
        else:
            for k in range(crossing):
                staged[c][k] = arrived[c][index[0, k]]
        swap(c).start()

    def collect_on(c):
        swap(c).wait_recv()
        for i in range(half):
            near = arrived[c][index[1, i]]
            far = swapped[c][index[2, i]]
            ordered[c][i] = jnp.where(index[3, i] == 1, near, far)
        stay_last(c).start()

        @pl.loop(1, half)
        def _(o):
            collect(c, o).start()

    r_orders = reduce_orders(p.expert_bits, p.dp_bits)
    r_flights = [[], []]

    def split(i, s):
        axis, bit = r_orders[i][s]
        if s == 0:
            ref, rows = part, pl.ds(i * rows_half, rows_half)
        else:
            ref, rows = sums[i][s - 1], slice(None)
        left = [b for a, b in r_orders[i][s:] if a == "expert"]
        left = sorted(left, reverse=True)
        if axis == "expert":
            mine = (e // 2**bit) % 2
            spot = left.index(bit)

            def where(v):
                return tuple(
                    [slice(None)] * spot + [v] + [slice(None)] * (len(left) - spot - 1)
                ) + (rows, slice(None))

            return ref, where(mine), where(1 - mine)
        mine = (d // 2**bit) % 2
        span = 2**bit * width
        head = (slice(None),) * len(left) + (rows,)
        keep = head + (pl.ds(pl.multiple_of(mine * span, LANES), span),)
        give = head + (pl.ds(pl.multiple_of((1 - mine) * span, LANES), span),)
        return ref, keep, give

    def start_step(i, s):
        ref, _, give = split(i, s)
        c = pltpu.make_async_remote_copy(
            src_ref=ref.at[give],
            dst_ref=came[i][s],
            send_sem=rsend.at[i, s],
            recv_sem=rrecv.at[i, s],
            device_id=peer(*r_orders[i][s]),
            device_id_type=MESH,
        )
        c.start()
        r_flights[i].append(c)

    def end_step(i, s):
        ref, keep, _ = split(i, s)
        r_flights[i][s].wait_recv()
        total = ref[keep].astype(jnp.float32) + came[i][s][...].astype(jnp.float32)
        sums[i][s][...] = total.astype(sums[i][s].dtype)

    def next_step(s):
        for i in range(halves):
            end_step(i, s)
            if s + 1 < steps:
                start_step(i, s + 1)

    def pack_rows(src, dst, w_ref):
        span = min(512, p.model)

        @pl.loop(0, p.model // span)
        def _(t):
            cols = pl.ds(pl.multiple_of(t * span, span), span)
            for g in range(p.groups):
                rows = slice(g * p.group_toks, (g + 1) * p.group_toks)
                at_rows = slice(g * p.group_slots, (g + 1) * p.group_slots)
                x = src[rows, cols]
                if w_ref is not None:
                    x = (x.astype(jnp.float32) * w_ref[rows, :][:, :1]).astype(jnp.bfloat16)
                x_rows[at_rows, :] = jnp.dot(
                    p_picks[g], x, preferred_element_type=jnp.float32
                ).astype(jnp.bfloat16)
            dst[cols, :] = jnp.transpose(x_rows[...])

    def make_part(first, last):
        tile = min(512, p.model)

        @pl.loop(first * p.model // (2 * tile), last * p.model // (2 * tile))
        def _(t):
            cols = pl.ds(pl.multiple_of(t * tile, tile), tile)
            piece = lax.dot_general(
                backs[0], w_gate[0, cols, :], contract_cols, preferred_element_type=jnp.float32
            )
            piece += lax.dot_general(
                backs[1], w_up[0, cols, :], contract_cols, preferred_element_type=jnp.float32
            )
            shape = part.shape[:-1] + (tile,)
            part[..., cols] = piece.astype(part.dtype).reshape(shape)

    for u in range(p.spans):
        first_half(u)
        begin(KINDS * u, 2, u)
        if u == 0:
            scale()
        second_half(u)
        begin(KINDS * u + 1, 0, u)
        begin(KINDS * u + 2, 1, u)
    make_part(0, 1)
    swap_on(0)
    make_part(1, 2)
    for i in range(halves):
        start_step(i, 0)
    for c in range(1, KINDS):
        swap_on(c)
    next_step(0)
    for c in range(KINDS, chunks):
        swap_on(c)
    for c in flights.values():
        c.wait_send()
    for c in meta_flights.values():
        c.wait_send()
    pack_rows(all_tok, x_cols, None)
    row_out = pltpu.make_async_copy(x_cols, out_rows, osem.at[0])
    row_out.start()
    pace = 42 * crossing / (half * chunks)
    events = [(10 + pace * (c + 1), 0, c) for c in range(chunks)]
    events += [(12 + 6.5 * s, 1, s) for s in range(1, steps)]
    events.append((10, 2, 0))
    for _, kind, which in sorted(events):
        if kind == 0:
            collect_on(which)
        elif kind == 1:
            next_step(which)
        else:
            pack_rows(all_cot, g_cols, p_weights)
            grad_out = pltpu.make_async_copy(g_cols, out_grads, osem.at[1])
            grad_out.start()
    for i in range(halves):
        summed[pl.ds(i * rows_half, rows_half), :] = sums[i][steps - 1][...]
    result_out = pltpu.make_async_copy(summed, result, osem.at[2])
    result_out.start()

    for f in r_flights:
        for c in f:
            c.wait_send()
    row_out.wait()
    grad_out.wait()
    result_out.wait()
    for c in range(chunks):
        stay_last(c).wait()
        swap(c).wait_send()

        @pl.loop(1, half)
        def _(o):
            spread(c, o).wait_send()
            collect(c, o).wait_send()
            collect(c, o).wait_recv()


def communicate(p, crossing, call_id, operands):
    dtype = operands[1].dtype
    reduce_buffers = []
    for order in reduce_orders(p.expert_bits, p.dp_bits):
        for shape in reduce_shapes(order, p.expert_bits, p.dp_bits, p.tok_rows // 2, p.width):
            reduce_buffers.append(pltpu.VMEM(shape, dtype))
    piece = (p.piece_rows, LANES)
    weight = operands[-1].shape
    dma = pltpu.SemaphoreType.DMA
    steps, chunks, half = p.steps, p.chunks, p.half
    scratch = (
        reduce_buffers
        + reduce_buffers
        + [pltpu.VMEM((half,) + piece, dtype)] * chunks
        + [pltpu.VMEM((crossing,) + piece, dtype)] * (2 * chunks)
        + [pltpu.VMEM((half,) + piece, dtype)] * chunks
        + [
            pltpu.VMEM((p.total, p.model), dtype),
            pltpu.VMEM((p.total, p.model), dtype),
            pltpu.VMEM((p.n_expert, p.top_count, p.tok_rows), jnp.int32),
            pltpu.VMEM((p.n_expert, p.top_count, p.tok_rows), jnp.float32),
            pltpu.VMEM(weight, dtype),
            pltpu.VMEM(weight, dtype),
            pltpu.VMEM(weight, dtype),
            pltpu.VMEM((p.total, LANES), jnp.float32),
            pltpu.VMEM((p.total, LANES), jnp.float32),
            pltpu.VMEM((p.groups, p.group_slots, p.group_toks), dtype),
            pltpu.VMEM((p.groups, p.group_slots, p.group_toks), dtype),
            pltpu.VMEM((p.total, p.span), jnp.float32),
            pltpu.VMEM((p.total, p.span), jnp.float32),
            pltpu.VMEM((KINDS, p.total, p.hidden), dtype),
            pltpu.VMEM((chunks, half) + piece, dtype),
            pltpu.SMEM((4, half), jnp.int32),
            pltpu.VMEM((2,) * p.expert_bits + (p.tok_rows, p.model), dtype),
            pltpu.VMEM((p.slots, min(512, p.model)), dtype),
            pltpu.VMEM((p.model, p.slots), dtype),
            pltpu.VMEM((p.model, p.slots), dtype),
            pltpu.VMEM((p.tok_rows, p.width), dtype),
            dma((2 * p.row_parts, 2**steps)),
            dma((2 * p.row_parts, 2**steps)),
            dma((2, p.n_expert)),
            dma((2, p.n_expert)),
            dma((4,)),
            dma((3,)),
            dma((chunks, half)),
            dma((chunks, half)),
            dma((chunks,)),
            dma((chunks,)),
            dma((chunks, half)),
            dma((chunks, half)),
            dma((chunks,)),
            dma((chunks,)),
            dma((2, steps)),
            dma((2, steps)),
            dma((3,)),
        ]
    )
    anywhere = pl.BlockSpec(memory_space=pl.ANY)
    return pl.pallas_call(
        functools.partial(comm_kernel, p, crossing),
        out_shape=(
            jax.ShapeDtypeStruct((chunks, half) + piece, dtype),
            jax.ShapeDtypeStruct((p.model, p.slots), dtype),
            jax.ShapeDtypeStruct((p.model, p.slots), dtype),
            jax.ShapeDtypeStruct((p.tok_rows, p.width), dtype),
        ),
        in_specs=[pl.BlockSpec(memory_space=pltpu.SMEM)] + [anywhere] * 7,
        out_specs=[anywhere] * 4,
        scratch_shapes=scratch,
        compiler_params=pltpu.CompilerParams(
            collective_id=call_id, has_side_effects=True, vmem_limit_bytes=64 * 2**20 - 2**16
        ),
    )(*operands)


def final_kernel(
    p, landed, rows, grads, summed, g_gate, g_up, g_down, out, items, x, g, small, acts, sums,
    item_sem, x_sem, g_sem, small_sem, out_sem,
):
    tile = min(512, p.model)
    count = p.model // tile
    item_in = pltpu.make_async_copy(landed, items, item_sem)
    item_in.start()

    def load(i):
        at = pl.ds(pl.multiple_of(i * tile, tile), tile)
        return (
            pltpu.make_async_copy(rows.at[at], x.at[at], x_sem.at[i]),
            pltpu.make_async_copy(grads.at[at], g.at[at], g_sem.at[i]),
        )

    def store(i):
        at = pl.ds(pl.multiple_of(i * tile, tile), tile)
        return [
            pltpu.make_async_copy(sums.at[k, at], dst.at[0, at], out_sem.at[k, i])
            for k, dst in enumerate((g_gate, g_up, g_down))
        ]

    for i in range(count):
        for c in load(i):
            c.start()
    small_in = pltpu.make_async_copy(summed, small, small_sem.at[0])
    small_in.start()
    item_in.wait()
    for u in range(p.spans):
        for i, kind in enumerate((2, 0, 1)):
            for t in range(p.col_tiles):
                at = u * p.span + t * LANES
                piece = items[KINDS * u + i, t * p.row_split : (t + 1) * p.row_split]
                acts[kind, :, at : at + LANES] = piece.reshape(p.padded, LANES)[: p.slots]
    small_in.wait()
    small_out = pltpu.make_async_copy(small, out, small_sem.at[1])
    small_out.start()

    @pl.loop(0, count)
    def _(i):
        at = pl.ds(pl.multiple_of(i * tile, tile), tile)
        for c in load(i):
            c.wait()
        outs = store(i)
        for k, src in enumerate((x, x, g)):
            sums[k, at, :] = jnp.dot(src[at, :], acts[k], preferred_element_type=jnp.float32)
            outs[k].start()

    small_out.wait()

    @pl.loop(0, count)
    def _(i):
        for c in store(i):
            c.wait()


def finish(p, landed, rows, grads, summed):
    tile = min(512, p.model)
    grad_shape = jax.ShapeDtypeStruct((1, p.model, p.hidden), jnp.float32)
    anywhere = pl.BlockSpec(memory_space=pl.ANY)
    dma = pltpu.SemaphoreType.DMA
    return pl.pallas_call(
        functools.partial(final_kernel, p),
        out_shape=(
            grad_shape,
            grad_shape,
            grad_shape,
            jax.ShapeDtypeStruct(summed.shape, summed.dtype),
        ),
        in_specs=[anywhere] * 4,
        out_specs=[anywhere] * 4,
        scratch_shapes=[
            pltpu.VMEM(landed.shape, landed.dtype),
            pltpu.VMEM(rows.shape, rows.dtype),
            pltpu.VMEM(grads.shape, grads.dtype),
            pltpu.VMEM(summed.shape, summed.dtype),
            pltpu.VMEM((KINDS, p.slots, p.hidden), landed.dtype),
            pltpu.VMEM((KINDS, p.model, p.hidden), jnp.float32),
            dma,
            dma((p.model // tile,)),
            dma((p.model // tile,)),
            dma((2,)),
            dma((KINDS, p.model // tile)),
        ],
    )(landed, rows, grads, summed)


def local(n_expert, n_dp, tokens, cotangent, routes, probs, matching, w_gate, w_up, w_down):
    tok_rows, top_count = routes.shape
    p = Plan(n_expert, n_dp, tok_rows, tokens.shape[1], top_count, w_gate.shape[2])
    operands = (matching, tokens, cotangent, routes.T, probs.T, w_gate, w_up, w_down)
    sizes = (p.half // 2, 3 * p.half // 4, p.half)
    low = jnp.arange(n_expert) < p.half
    crossed = jnp.sum((low != (matching < p.half)).astype(jnp.int32))
    over = jnp.maximum(crossed - (p.half // 2 + 1), 0)
    which = lax.shift_right_logical(over, bit_count(p.half // 2))
    calls = [
        functools.partial(lambda size, i, *a: communicate(p, size, i, a), size, i)
        for i, size in enumerate(sizes)
    ]
    landed, rows, grads, summed = lax.switch(which, calls, *operands)
    g_gate, g_up, g_down, input_grad = finish(p, landed, rows, grads, summed)
    return input_grad, g_gate, g_up, g_down


def solution(mesh):
    weights = P("expert", None, "dp")
    return jax.shard_map(
        functools.partial(local, mesh.shape["expert"], mesh.shape["dp"]),
        mesh=mesh,
        in_specs=(
            P("expert", "dp"),
            P("expert", "dp"),
            P("expert", None),
            P("expert", None),
            P(),
            weights,
            weights,
            weights,
        ),
        out_specs=(P("expert", "dp"), weights, weights, weights),
        check_vma=False,
    )
```
